32 devices in a mesh: cp: 8 (over z, y), ep: 4 (over x, core).
Axes of the slice: x: 2, y: 2, z: 4, core: 2. Of those that a mesh axis runs over, the one named last changes fastest.
Arguments:
- residual: bfloat16 [1024, 6144], P('cp'), may hold values from -90 to 90
- queries: bfloat16 [1024, 3072], P('cp', 'ep'), may hold values from -256 to 256
- key_proj: bfloat16 [1024, 512], P('cp', 'ep'), may hold values from -8 to 8
- value_proj: bfloat16 [1024, 512], P('cp', 'ep'), may hold values from -12 to 12
- out_weight: bfloat16 [3072, 6144], P('ep'), may hold values from -0.109375 to 0.109375
- norm_gain: float32 [6144], replicated, may hold values from 0.1 to 1.9
- doc_ids: int32 [1024], replicated, may hold values from 0 to 11, never falling along the last dimension, each value on 1 to 256 neighbouring positions
- block_order: int32 [8], replicated, may hold values from 0 to 7, each once
- expert_ids: int32 [1024, 2], P('cp'), may hold values from 0 to 7, as said below
- route_logits: float32 [1024, 2], P('cp'), may hold values from -12 to 12
- gate_weight: bfloat16 [4, 6144, 8192], P('ep', None, 'cp'), may hold values from -0.078125 to 0.078125
- up_weight: bfloat16 [4, 6144, 8192], P('ep', None, 'cp'), may hold values from -0.078125 to 0.078125
- down_weight: bfloat16 [4, 8192, 6144], P('ep', 'cp'), may hold values from -0.0625 to 0.0625
Outputs:
- hidden_state: bfloat16 [1024, 6144], P('cp', 'ep')
- expert_mix: bfloat16 [1024, 6144], P('cp', 'ep')
The draws below stay inside these ranges and needn't reach their ends.
Inputs may be any that keep to these rules, and one draw needn't show every extreme that they name: `expert_ids`: each row names two different experts; within the 128 rows of one cp index no expert is named by more than 40 rows. `doc_ids`: document numbers never fall along the sequence. `block_order`: each block number appears once.
All inputs are finite; a program needn't handle non-finite values.
Results may differ from the reference program's by a relative error of at most 0.02.
Values may be sent and summed in bfloat16 or wider, within the bound.
A program may use at most 128 MiB of HBM per device.

```python
import math
import jax
import jax.numpy as jnp
import numpy as np
from jax import lax

D = 6144
HD = 128
EXPERTS = 8
QH = 24
KVH = 4
FFW = 8192
DOCS = 12
TOK_DEV = 128
SEQ = 1024
CAP = 40
EXP_WIN = 4
N_CP = 8


def key_base(key):
    return jax.random.truncated_normal(jax.random.fold_in(key, 31), -6.0, 6.0, (SEQ, KVH, HD), jnp.float32)


def draw_key_proj(key, part):
    base = key_base(key)
    return base.reshape(SEQ, KVH * HD).astype(jnp.bfloat16)


def draw_queries(key, part):
    base = jax.random.truncated_normal(jax.random.fold_in(key, 41), -6.0, 6.0, (SEQ, QH, HD), jnp.float32)
    return base.reshape(SEQ, QH * HD).astype(jnp.bfloat16)


def draw_residual(key, part):
    base = jax.random.truncated_normal(jax.random.fold_in(key, 21), -6.0, 6.0, (SEQ, D), jnp.float32)
    return base.astype(jnp.bfloat16)


def draw_expert_ids(key, part):
    blocks = SEQ // TOK_DEV
    filled = jax.random.randint(jax.random.fold_in(key, 3), (), 0, EXP_WIN, dtype=jnp.int32)
    others = EXPERTS - 2
    remaining = 2 * TOK_DEV - 2 * CAP
    expert_range = jnp.arange(EXPERTS, dtype=jnp.int32)
    entry_range = jnp.arange(2 * TOK_DEV, dtype=jnp.int32)

    def one_block(block_key):
        first_key, second_key, third_key, fourth_key = jax.random.split(block_key, 4)
        second = (filled + 1 + jax.random.randint(first_key, (), 0, EXPERTS - 1, dtype=jnp.int32)) % EXPERTS
        is_top = (expert_range == filled) | (expert_range == second)
        other_rank = jnp.clip(jnp.cumsum(1 - is_top.astype(jnp.int32)) - 1, 0, others - 1)
        ordering = jax.random.permutation(second_key, others)
        extra = (ordering[other_rank] < remaining % others).astype(jnp.int32)
        counts = jnp.where(is_top, CAP, remaining // others + extra).astype(jnp.int32)
        bounds = jnp.cumsum(counts)
        entries = jnp.sum((entry_range[:, None] >= bounds[None, :]).astype(jnp.int32), axis=1)
        paired = jnp.stack([entries[:TOK_DEV], entries[TOK_DEV:]], axis=1)
        paired = paired[jax.random.permutation(third_key, TOK_DEV)]
        flipped = jax.random.randint(fourth_key, (TOK_DEV, 1), 0, 2, dtype=jnp.int32)
        return jnp.where(flipped == 1, paired[:, ::-1], paired)
    block_keys = jax.random.split(jax.random.fold_in(key, 5), blocks)
    return jax.vmap(one_block)(block_keys).reshape(SEQ, 2).astype(jnp.int32)


def shard_levels(rng, dims, pieces, low, top_value):
    level, own = 1.0, jax.random.fold_in(rng, 6)
    for axis_at, shards_of in pieces:
        heights = jnp.exp(jax.random.uniform(jax.random.fold_in(own, axis_at), (shards_of,), jnp.float32, low / len(pieces), top_value / len(pieces)))
        level = level * jnp.repeat(heights, dims[axis_at] // shards_of).reshape([-1 if axis == axis_at else 1 for axis in range(len(dims))])
    return level


def length_profile(number_of, total, most, slope):
    weights = [(1 << 20) // math.isqrt(grade ** slope) + 1 for grade in range(2, number_of + 1)]
    surplus, given = total - most - (number_of - 1), [1] * (number_of - 1)
    while surplus > 0:
        movable = [i for i in range(number_of - 1) if given[i] < most]
        mass, budget = sum([weights[i] for i in movable]), surplus
        for i in movable:
            more = min(most - given[i], max(1, budget * weights[i] // mass), surplus)
            given[i] = given[i] + more
            surplus = surplus - more
    return np.array([most] + given)


def ragged(own_key, amount, total, bound, skew):
    if amount == 2:
        one = jax.random.randint(own_key, (), max(1, total - bound), min(bound, total - 1) + 1)
        return jnp.stack([one, total - one])
    tallies = jnp.asarray(length_profile(amount, total, bound, skew), jnp.int32)
    pairs = (amount - 1) // 2
    donor, sink = tallies[1:1 + 2 * pairs:2], tallies[2:2 + 2 * pairs:2]
    room = jnp.minimum(donor - 1, bound - sink)
    passed = jax.random.randint(jax.random.fold_in(own_key, 1), (pairs,), 0, 1 << 20) % (room + 1)
    tallies = tallies.at[1:1 + 2 * pairs:2].set(donor - passed).at[2:2 + 2 * pairs:2].set(sink + passed)
    return tallies[jax.random.permutation(jax.random.fold_in(own_key, 2), amount)]


def centred(key, shape, width, limit, cuts=(), kind=jnp.bfloat16):
    loudness = shard_levels(key, shape, cuts, -0.22, 0.18) if cuts else 1.0
    values = jax.random.normal(key, shape, jnp.float32) * width * loudness
    return jnp.minimum(jnp.maximum(values, -limit), limit).astype(kind)


def setup_inputs(seed: int = 0) -> dict:
    key_list = jax.random.split(jax.random.key(seed), 14)
    residual = draw_residual(jax.random.fold_in(key_list[13], 71), 0)
    queries = draw_queries(jax.random.fold_in(key_list[13], 71), 0)
    key_proj = draw_key_proj(jax.random.fold_in(key_list[13], 71), 0)
    value_proj = centred(key_list[3], (SEQ, KVH * HD), 2.0, 12.0, ((0, 8), (1, 4)))
    out_weight = centred(key_list[4], (QH * HD, D), (QH * HD) ** -0.5, 0.109375, ((0, 4),))
    norm_gain = jnp.clip(1.0 + 0.18 * jax.random.normal(key_list[5], (D,), jnp.float32), 0.1, 1.9)
    doc_ids = jnp.searchsorted(jnp.cumsum(ragged(key_list[6], DOCS, SEQ, SEQ // 4, 2)), jnp.arange(SEQ), side="right").astype(jnp.int32)
    block_order = jax.random.permutation(key_list[7], N_CP).astype(jnp.int32)
    expert_ids = draw_expert_ids(jax.random.fold_in(key_list[13], 71), 0)
    route_logits = centred(key_list[9], (SEQ, 2), 2.0, 12.0, ((0, 8),), jnp.float32)
    gate_weight = centred(key_list[10], (EXP_WIN, D, FFW), D ** -0.5, 0.078125, ((0, 4), (2, 8)))
    up_weight = centred(key_list[11], (EXP_WIN, D, FFW), D ** -0.5, 0.078125, ((0, 4), (2, 8)))
    down_weight = centred(key_list[12], (EXP_WIN, FFW, D), FFW ** -0.5, 0.0625, ((0, 4), (1, 8)))
    return {"residual": residual, "queries": queries, "key_proj": key_proj, "value_proj": value_proj, "out_weight": out_weight, "norm_gain": norm_gain, "doc_ids": doc_ids, "block_order": block_order, "expert_ids": expert_ids, "route_logits": route_logits, "gate_weight": gate_weight, "up_weight": up_weight, "down_weight": down_weight}


EPS = 1e-05
NEG = -1e+30

def reference(residual, queries, key_proj, value_proj, out_weight, norm_gain, doc_ids, block_order, expert_ids, route_logits, gate_weight, up_weight, down_weight):
    positions = (block_order[:, None] * TOK_DEV + jnp.arange(TOK_DEV, dtype=jnp.int32)[None, :]).reshape(SEQ).astype(jnp.int32)
    row_docs = jnp.take(doc_ids, positions)
    allowed = (row_docs[:, None] == row_docs[None, :]) & (positions[None, :] <= positions[:, None])
    group_size = QH // KVH
    score_scale = 1.0 / math.sqrt(HD)
    query_heads = queries.reshape(SEQ, QH, HD)
    key_heads = key_proj.reshape(SEQ, KVH, HD)
    value_heads = value_proj.reshape(SEQ, KVH, HD)

    def one_head(head_index):
        query_rows = lax.dynamic_index_in_dim(query_heads, head_index, 1, keepdims=False)
        key_rows = lax.dynamic_index_in_dim(key_heads, head_index // group_size, 1, keepdims=False)
        value_rows = lax.dynamic_index_in_dim(value_heads, head_index // group_size, 1, keepdims=False)
        scores = lax.dot_general(query_rows, key_rows, (((1,), (1,)), ((), ())), preferred_element_type=jnp.float32) * score_scale
        scores = jnp.where(allowed, scores, NEG)
        row_max = lax.optimization_barrier(jnp.max(scores, axis=1, keepdims=True))
        weights = jnp.where(allowed, jnp.exp(scores - row_max), 0.0)
        row_total = lax.optimization_barrier(jnp.sum(weights, axis=1, keepdims=True))
        value_mix = jnp.dot(weights.astype(jnp.bfloat16), value_rows, preferred_element_type=jnp.float32)
        return value_mix / row_total
    attended = lax.map(one_head, jnp.arange(QH, dtype=jnp.int32))
    attended = attended.transpose(1, 0, 2).reshape(SEQ, QH * HD).astype(jnp.bfloat16)
    projected = jnp.dot(attended, out_weight, preferred_element_type=jnp.float32)
    hidden_state = (residual.astype(jnp.float32) + projected).astype(jnp.bfloat16)
    values_wide = hidden_state.astype(jnp.float32)
    mean_square = lax.optimization_barrier(jnp.mean(values_wide * values_wide, axis=1, keepdims=True))
    normed = (values_wide * lax.rsqrt(mean_square + EPS) * norm_gain).astype(jnp.bfloat16)
    logit_gap = route_logits[:, 1] - route_logits[:, 0]
    first_share = 1.0 / (1.0 + jnp.exp(logit_gap))
    second_share = 1.0 / (1.0 + jnp.exp(-logit_gap))
    slice_width = FFW // N_CP
    block_normed = normed.reshape(N_CP, TOK_DEV, D).astype(jnp.float32)
    slot_ids = jnp.arange(CAP, dtype=jnp.int32)
    block_base = jnp.arange(SEQ, dtype=jnp.int32) // TOK_DEV * CAP
    mixture = jnp.zeros((SEQ, D), jnp.float32)
    for expert in range(EXP_WIN):
        is_member = ((expert_ids[:, 0] == expert) | (expert_ids[:, 1] == expert)).astype(jnp.int32)
        member_blocks = is_member.reshape(N_CP, TOK_DEV)
        slot_index = jnp.cumsum(member_blocks, axis=1) - member_blocks
        selector = ((slot_index[:, None, :] == slot_ids[None, :, None]) & (member_blocks[:, None, :] == 1)).astype(jnp.float32)
        packed = jnp.einsum('bct,btd->bcd', selector, block_normed).astype(jnp.bfloat16).reshape(N_CP * CAP, D)
        gated = jnp.dot(packed, gate_weight[expert], preferred_element_type=jnp.float32)
        lifted = jnp.dot(packed, up_weight[expert], preferred_element_type=jnp.float32)
        hidden = (jax.nn.silu(gated) * lifted).astype(jnp.bfloat16)
        hidden_slices = hidden.reshape(N_CP * CAP, N_CP, slice_width).transpose(1, 0, 2)
        down_slices = down_weight[expert].reshape(N_CP, slice_width, D)

        def add_slice(running, pair):
            term = jnp.dot(pair[0], pair[1], preferred_element_type=jnp.float32).astype(jnp.bfloat16)
            term = lax.optimization_barrier(term)
            return (running + term.astype(jnp.float32), None)
        expert_sum, unused = lax.scan(add_slice, jnp.zeros((N_CP * CAP, D), jnp.float32), (hidden_slices, down_slices))
        route_share = jnp.where(expert_ids[:, 0] == expert, first_share, 0.0) + jnp.where(expert_ids[:, 1] == expert, second_share, 0.0)
        row_index = (block_base + jnp.minimum(slot_index.reshape(SEQ), CAP - 1)).astype(jnp.int32)
        mixture = mixture + jnp.take(expert_sum, row_index, axis=0) * route_share[:, None]
    return (hidden_state, mixture.astype(jnp.bfloat16))
```

```python
import functools
import math

import jax
import jax.numpy as jnp
from jax import lax
from jax.experimental import pallas as pl
from jax.experimental.pallas import tpu as pltpu
from jax.sharding import PartitionSpec as P

HD = 128
CAP = 40


EPS = 1e-05
NEG = -1e30
VMEM = pl.BlockSpec(memory_space=pltpu.VMEM)
ANY = pl.BlockSpec(memory_space=pl.ANY)


def cp_place(n):
    me = lax.axis_index("cp")
    low = lax.rem(me, 2)
    return me, me // 2, low, me + 1 - 2 * low, n // 2


def greet(n, ep_count):
    me, high, low, partner, m = cp_place(n)
    barrier = pltpu.get_barrier_semaphore()
    pl.semaphore_signal(barrier, inc=1, device_id={"cp": partner})
    for d in range(1, m):
        peer = lax.rem(high + d, m) * 2 + low
        pl.semaphore_signal(barrier, inc=1, device_id={"cp": peer})
    ep = lax.axis_index("ep")
    for d in range(1, ep_count):
        pl.semaphore_signal(barrier, inc=1, device_id={"ep": lax.rem(ep + d, ep_count)})
    pl.semaphore_wait(barrier, m + ep_count - 1)


def gather_blocks(n, block, out_ref, send_sem, recv_sem, local_sem):
    me, high, low, partner, m = cp_place(n)

    def copy(src, index, sem_at, peer):
        return pltpu.make_async_remote_copy(
            src_ref=src,
            dst_ref=out_ref.at[index],
            send_sem=send_sem.at[sem_at],
            recv_sem=recv_sem.at[sem_at],
            device_id={"cp": peer},
        )

    own = pltpu.make_async_copy(block, out_ref.at[me], local_sem)
    own.start()
    sent = []
    for d in range(1, m):
        c = copy(block, me, d, lax.rem(high + d, m) * 2 + low)
        c.start()
        sent.append(c)
    c = copy(block, me, 0, partner)
    c.start()
    sent.append(c)
    for d in range(1, m):
        source = lax.rem(high + m - d, m) * 2 + low
        copy(block, source, d, partner).wait_recv()
        c = copy(out_ref.at[source], source, m - 1 + d, partner)
        c.start()
        sent.append(c)
    copy(block, partner, 0, partner).wait_recv()
    for d in range(1, m):
        source = lax.rem(high + m - d, m) * 2 + 1 - low
        copy(block, source, m - 1 + d, partner).wait_recv()
    for c in sent:
        c.wait_send()
    own.wait()


def gather_kernel(n, x_ref, out_ref, send_sem, recv_sem, local_sem):
    greet(n, 1)
    gather_blocks(n, x_ref, out_ref, send_sem, recv_sem, local_sem)


def gather_call(x, n):
    count = 2 * (n // 2) - 1
    return pl.pallas_call(
        functools.partial(gather_kernel, n),
        out_shape=jax.ShapeDtypeStruct((n, *x.shape), x.dtype),
        in_specs=[VMEM],
        out_specs=ANY,
        scratch_shapes=[
            pltpu.SemaphoreType.DMA((count,)),
            pltpu.SemaphoreType.DMA((count,)),
            pltpu.SemaphoreType.DMA,
        ],
        compiler_params=pltpu.CompilerParams(
            collective_id=0, has_side_effects=True, vmem_limit_bytes=4 << 20
        ),
        name="kv_gather",
    )(x)


def ep_exchange(ep_count, source_of, target_of, send_sem, recv_sem):
    ep = lax.axis_index("ep")
    copies = []
    for d in range(1, ep_count):
        peer = lax.rem(ep + d, ep_count)
        c = pltpu.make_async_remote_copy(
            src_ref=source_of(peer),
            dst_ref=target_of(ep, d),
            send_sem=send_sem.at[d - 1],
            recv_sem=recv_sem.at[d - 1],
            device_id={"ep": peer},
        )
        c.start()
        copies.append(c)
    return copies


def route_kernel(
    n, ep_count, terms_ref, residual_ref, selector_ref, gain_ref,
    hidden_ref, gathered_ref,
    landed, chosen, raw, block,
    term_send, term_recv, row_send, row_recv, send_sem, recv_sem, local_sem,
):
    greet(n, ep_count)
    ep = lax.axis_index("ep")
    width = hidden_ref.shape[1]
    features = width * ep_count

    def share_of(ref, index):
        return ref.at[:, pl.ds(pl.multiple_of(index * width, 128), width)]

    copies = ep_exchange(
        ep_count,
        lambda peer: share_of(terms_ref, peer),
        lambda me, d: landed.at[d - 1],
        term_send,
        term_recv,
    )
    total = share_of(residual_ref, ep)[...].astype(jnp.float32) + share_of(terms_ref, ep)[
        ...
    ].astype(jnp.float32)
    for d, c in enumerate(copies):
        c.wait()
        total = total + landed[d].astype(jnp.float32)
    hidden = total.astype(jnp.bfloat16)
    hidden_ref[...] = hidden
    for e in range(ep_count):
        chosen[e] = jnp.dot(
            selector_ref[e], hidden, preferred_element_type=jnp.float32
        ).astype(jnp.bfloat16)
    copies = ep_exchange(
        ep_count, lambda peer: chosen.at[peer], lambda me, d: raw.at[me], row_send, row_recv
    )
    raw[ep] = chosen[ep]
    for c in copies:
        c.wait()
    squares = jnp.zeros((block.shape[0], 1), jnp.float32)
    for q in range(ep_count):
        wide = raw[q].astype(jnp.float32)
        squares = squares + jnp.sum(wide * wide, axis=1, keepdims=True)
    scale = lax.rsqrt(squares / features + EPS)
    for q in range(ep_count):
        columns = slice(q * width, (q + 1) * width)
        block[:, columns] = (raw[q].astype(jnp.float32) * scale * gain_ref[:, columns]).astype(
            jnp.bfloat16
        )
    gather_blocks(n, block, gathered_ref, send_sem, recv_sem, local_sem)


def route_call(terms, residual, selector, gain, n, ep_count):
    tokens, features = terms.shape
    width = features // ep_count
    count = 2 * (n // 2) - 1
    dma = pltpu.SemaphoreType.DMA
    return pl.pallas_call(
        functools.partial(route_kernel, n, ep_count),
        out_shape=(
            jax.ShapeDtypeStruct((tokens, width), jnp.bfloat16),
            jax.ShapeDtypeStruct((n, CAP, features), jnp.bfloat16),
        ),
        in_specs=[VMEM] * 4,
        out_specs=(VMEM, ANY),
        scratch_shapes=[
            pltpu.VMEM((ep_count - 1, tokens, width), jnp.bfloat16),
            pltpu.VMEM((ep_count, CAP, width), jnp.bfloat16),
            pltpu.VMEM((ep_count, CAP, width), jnp.bfloat16),
            pltpu.VMEM((CAP, features), jnp.bfloat16),
            dma((ep_count - 1,)),
            dma((ep_count - 1,)),
            dma((ep_count - 1,)),
            dma((ep_count - 1,)),
            dma((count,)),
            dma((count,)),
            dma,
        ],
        compiler_params=pltpu.CompilerParams(
            collective_id=1, has_side_effects=True, vmem_limit_bytes=16 << 20
        ),
        name="route",
    )(terms, residual, selector, gain)


def combine_kernel(
    n, ep_count, partial_ref, placer_ref, share_ref, out_ref,
    near, passed, far, sums, slots,
    near_send, near_recv, far_send, far_recv, slot_send, slot_recv,
):
    greet(n, ep_count)
    me, high, low, partner, m = cp_place(n)
    ep = lax.axis_index("ep")
    width = out_ref.shape[1]
    near_copies = []
    for d in [*range(1, m), 0]:
        c = pltpu.make_async_remote_copy(
            src_ref=partial_ref.at[lax.rem(high + d, m) * 2 + 1 - low],
            dst_ref=near.at[d],
            send_sem=near_send.at[d],
            recv_sem=near_recv.at[d],
            device_id={"cp": partner},
        )
        c.start()
        near_copies.append(c)
    far_copies = []
    for d in range(1, m):
        near_copies[d - 1].wait_recv()
        target = lax.rem(high + d, m) * 2 + low
        for q in range(ep_count):
            columns = slice(q * width, (q + 1) * width)
            passed[d - 1, :, columns] = (
                partial_ref[target, :, columns].astype(jnp.float32)
                + near[d, :, columns].astype(jnp.float32)
            ).astype(jnp.bfloat16)
        c = pltpu.make_async_remote_copy(
            src_ref=passed.at[d - 1],
            dst_ref=far.at[d - 1],
            send_sem=far_send.at[d - 1],
            recv_sem=far_recv.at[d - 1],
            device_id={"cp": target},
        )
        c.start()
        far_copies.append(c)
    near_copies[m - 1].wait_recv()
    for c in far_copies:
        c.wait_recv()
    for q in range(ep_count):
        columns = slice(q * width, (q + 1) * width)
        total = partial_ref[me, :, columns].astype(jnp.float32) + near[0, :, columns].astype(
            jnp.float32
        )
        for d in range(1, m):
            total = total + far[d - 1, :, columns].astype(jnp.float32)
        sums[q] = total.astype(jnp.bfloat16)
    copies = ep_exchange(
        ep_count, lambda peer: sums.at[peer], lambda mine, d: slots.at[mine], slot_send, slot_recv
    )
    slots[ep] = sums[ep]
    for c in copies:
        c.wait()
    mix = jnp.zeros(out_ref.shape, jnp.float32)
    for e in range(ep_count):
        mix = mix + share_ref[e] * jnp.dot(
            placer_ref[e], slots[e], preferred_element_type=jnp.float32
        )
    out_ref[...] = mix.astype(jnp.bfloat16)
    for c in near_copies + far_copies:
        c.wait_send()


def combine_call(partial, placer, share, n, ep_count):
    features = partial.shape[2]
    tokens = placer.shape[1]
    width = features // ep_count
    m = n // 2
    dma = pltpu.SemaphoreType.DMA
    block_bytes = 2 * 48 * features
    return pl.pallas_call(
        functools.partial(combine_kernel, n, ep_count),
        out_shape=jax.ShapeDtypeStruct((tokens, width), jnp.bfloat16),
        in_specs=[VMEM] * 3,
        out_specs=VMEM,
        scratch_shapes=[
            pltpu.VMEM((m, CAP, features), jnp.bfloat16),
            pltpu.VMEM((m - 1, CAP, features), jnp.bfloat16),
            pltpu.VMEM((m - 1, CAP, features), jnp.bfloat16),
            pltpu.VMEM((ep_count, CAP, width), jnp.bfloat16),
            pltpu.VMEM((ep_count, CAP, width), jnp.bfloat16),
            dma((m,)),
            dma((m,)),
            dma((m - 1,)),
            dma((m - 1,)),
            dma((ep_count - 1,)),
            dma((ep_count - 1,)),
        ],
        compiler_params=pltpu.CompilerParams(
            collective_id=2,
            has_side_effects=True,
            vmem_limit_bytes=(n + 3 * m) * block_bytes + (8 << 20),
        ),
        name="combine",
    )(partial, placer, share)


def expert_hidden(rows_in, gate_weight, up_weight):
    gated = jnp.dot(rows_in, gate_weight[0], preferred_element_type=jnp.float32)
    lifted = jnp.dot(rows_in, up_weight[0], preferred_element_type=jnp.float32)
    return (jax.nn.silu(gated) * lifted).astype(jnp.bfloat16)


def local(
    residual,
    queries,
    key_proj,
    value_proj,
    out_weight,
    norm_gain,
    doc_ids,
    block_order,
    expert_ids,
    route_logits,
    gate_weight,
    up_weight,
    down_weight,
):
    tokens, features = residual.shape
    group_size = queries.shape[1] // HD
    score_scale = 1.0 / math.sqrt(HD)
    cp_rank = lax.axis_index("cp")
    n = lax.axis_size("cp")
    ep_count = lax.axis_size("ep")

    pairs = gather_call(jnp.concatenate([key_proj, value_proj], axis=1), n)
    pairs = pairs.reshape(n * tokens, 2 * HD)
    all_keys, all_values = pairs[:, :HD], pairs[:, HD:]
    row = jnp.arange(tokens, dtype=jnp.int32)
    all_pos = (block_order[:, None] * tokens + row[None, :]).reshape(n * tokens)
    all_docs = jnp.take(doc_ids.reshape(n, tokens), block_order, axis=0).reshape(n * tokens)
    placed = lax.dynamic_slice_in_dim(block_order, cp_rank, 1)[0]
    own_pos = placed * tokens + row
    own_docs = lax.dynamic_slice_in_dim(doc_ids, placed * tokens, tokens)
    allowed = (all_docs[None, :] == own_docs[:, None]) & (all_pos[None, :] <= own_pos[:, None])

    query_rows = queries.reshape(tokens * group_size, HD)
    scores = lax.dot_general(
        query_rows, all_keys, (((1,), (1,)), ((), ())), preferred_element_type=jnp.float32
    )
    scores = scores.reshape(tokens, group_size, n * tokens) * score_scale
    scores = jnp.where(allowed[:, None, :], scores, NEG)
    row_max = jnp.max(scores, axis=2)
    weights = jnp.where(allowed[:, None, :], jnp.exp(scores - row_max[:, :, None]), 0.0)
    row_total = jnp.sum(weights, axis=2)
    value_mix = jnp.dot(
        weights.astype(jnp.bfloat16).reshape(tokens * group_size, n * tokens),
        all_values,
        preferred_element_type=jnp.float32,
    ).reshape(tokens, group_size, HD)
    attended = (value_mix / row_total[:, :, None]).reshape(tokens, group_size * HD)
    projected = jnp.dot(
        attended.astype(jnp.bfloat16), out_weight, preferred_element_type=jnp.float32
    ).astype(jnp.bfloat16)

    logit_gap = route_logits[:, 1] - route_logits[:, 0]
    first_share = 1.0 / (1.0 + jnp.exp(logit_gap))
    second_share = 1.0 / (1.0 + jnp.exp(-logit_gap))
    experts = jnp.arange(ep_count, dtype=jnp.int32)[:, None] * gate_weight.shape[0]
    is_first = expert_ids[None, :, 0] == experts
    is_second = expert_ids[None, :, 1] == experts
    member = (is_first | is_second).astype(jnp.int32)
    slot = jnp.cumsum(member, axis=1) - member
    slot_ids = jnp.arange(CAP, dtype=jnp.int32)
    selector = (
        (slot[:, None, :] == slot_ids[None, :, None]) & (member[:, None, :] == 1)
    ).astype(jnp.bfloat16)
    placer = (
        (slot[:, :, None] == slot_ids[None, None, :]) & (member[:, :, None] == 1)
    ).astype(jnp.bfloat16)
    share = jnp.where(is_first, first_share[None], 0.0) + jnp.where(
        is_second, second_share[None], 0.0
    )

    hidden_state, packed = route_call(
        projected, residual, selector, norm_gain.reshape(1, features), n, ep_count
    )
    hidden = expert_hidden(packed.reshape(n * CAP, features), gate_weight, up_weight)
    terms = jnp.dot(hidden, down_weight[0], preferred_element_type=jnp.float32)
    terms = terms.astype(jnp.bfloat16).reshape(n, CAP, features)
    expert_mix = combine_call(terms, placer, share[:, :, None], n, ep_count)
    return (hidden_state, expert_mix)


def solution(mesh):
    return jax.shard_map(
        local,
        mesh=mesh,
        in_specs=(
            P("cp", None),
            P("cp", "ep"),
            P("cp", "ep"),
            P("cp", "ep"),
            P("ep", None),
            P(),
            P(),
            P(),
            P("cp", None),
            P("cp", None),
            P("ep", None, "cp"),
            P("ep", None, "cp"),
            P("ep", "cp", None),
        ),
        out_specs=(P("cp", "ep"), P("cp", "ep")),
        check_vma=False,
    )
```

```python
import functools
import math

import jax
import jax.numpy as jnp
from jax import lax
from jax.experimental import pallas as pl
from jax.experimental.pallas import tpu as pltpu
from jax.sharding import PartitionSpec as P

HD = 128
CAP = 40


EPS = 1e-05
NEG = -1e30
VMEM = pl.BlockSpec(memory_space=pltpu.VMEM)
ANY = pl.BlockSpec(memory_space=pl.ANY)


def cp_place(n):
    me = lax.axis_index("cp")
    low = lax.rem(me, 2)
    return me, me // 2, low, me + 1 - 2 * low, n // 2


def greet(n, ep_count):
    me, high, low, partner, m = cp_place(n)
    barrier = pltpu.get_barrier_semaphore()
    pl.semaphore_signal(barrier, inc=1, device_id={"cp": partner})
    for d in range(1, m):
        peer = lax.rem(high + d, m) * 2 + low
        pl.semaphore_signal(barrier, inc=1, device_id={"cp": peer})
    ep = lax.axis_index("ep")
    for d in range(1, ep_count):
        pl.semaphore_signal(barrier, inc=1, device_id={"ep": lax.rem(ep + d, ep_count)})
    pl.semaphore_wait(barrier, m + ep_count - 1)


def gather_blocks(n, block, out_ref, send_sem, recv_sem, local_sem):
    me, high, low, partner, m = cp_place(n)

    def copy(src, index, sem_at, peer):
        return pltpu.make_async_remote_copy(
            src_ref=src,
            dst_ref=out_ref.at[index],
            send_sem=send_sem.at[sem_at],
            recv_sem=recv_sem.at[sem_at],
            device_id={"cp": peer},
        )

    own = pltpu.make_async_copy(block, out_ref.at[me], local_sem)
    own.start()
    sent = []
    for d in range(1, m):
        c = copy(block, me, d, lax.rem(high + d, m) * 2 + low)
        c.start()
        sent.append(c)
    c = copy(block, me, 0, partner)
    c.start()
    sent.append(c)
    for d in range(1, m):
        source = lax.rem(high + m - d, m) * 2 + low
        copy(block, source, d, partner).wait_recv()
        c = copy(out_ref.at[source], source, m - 1 + d, partner)
        c.start()
        sent.append(c)
    copy(block, partner, 0, partner).wait_recv()
    for d in range(1, m):
        source = lax.rem(high + m - d, m) * 2 + 1 - low
        copy(block, source, m - 1 + d, partner).wait_recv()
    for c in sent:
        c.wait_send()
    own.wait()


def gather_kernel(n, x_ref, out_ref, send_sem, recv_sem, local_sem):
    greet(n, 1)
    gather_blocks(n, x_ref, out_ref, send_sem, recv_sem, local_sem)


def gather_call(x, n):
    count = 2 * (n // 2) - 1
    return pl.pallas_call(
        functools.partial(gather_kernel, n),
        out_shape=jax.ShapeDtypeStruct((n, *x.shape), x.dtype),
        in_specs=[VMEM],
        out_specs=ANY,
        scratch_shapes=[
            pltpu.SemaphoreType.DMA((count,)),
            pltpu.SemaphoreType.DMA((count,)),
            pltpu.SemaphoreType.DMA,
        ],
        compiler_params=pltpu.CompilerParams(
            collective_id=0, has_side_effects=True, vmem_limit_bytes=4 << 20
        ),
        name="kv_gather",
    )(x)


def ep_exchange(ep_count, source_of, target_of, send_sem, recv_sem):
    ep = lax.axis_index("ep")
    copies = []
    for d in range(1, ep_count):
        peer = lax.rem(ep + d, ep_count)
        c = pltpu.make_async_remote_copy(
            src_ref=source_of(peer),
            dst_ref=target_of(ep, d),
            send_sem=send_sem.at[d - 1],
            recv_sem=recv_sem.at[d - 1],
            device_id={"ep": peer},
        )
        c.start()
        copies.append(c)
    return copies


def route_kernel(
    n, ep_count, terms_ref, residual_ref, selector_ref, gain_ref,
    hidden_ref, gathered_ref,
    landed, chosen, raw, block,
    term_send, term_recv, row_send, row_recv, send_sem, recv_sem, local_sem,
):
    greet(n, ep_count)
    ep = lax.axis_index("ep")
    width = hidden_ref.shape[1]
    features = width * ep_count

    def share_of(ref, index):
        return ref.at[:, pl.ds(pl.multiple_of(index * width, 128), width)]

    copies = ep_exchange(
        ep_count,
        lambda peer: share_of(terms_ref, peer),
        lambda me, d: landed.at[d - 1],
        term_send,
        term_recv,
    )
    total = share_of(residual_ref, ep)[...].astype(jnp.float32) + share_of(terms_ref, ep)[
        ...
    ].astype(jnp.float32)
    for d, c in enumerate(copies):
        c.wait()
        total = total + landed[d].astype(jnp.float32)
    hidden = total.astype(jnp.bfloat16)
    hidden_ref[...] = hidden
    for e in range(ep_count):
        chosen[e] = jnp.dot(
            selector_ref[e], hidden, preferred_element_type=jnp.float32
        ).astype(jnp.bfloat16)
    copies = ep_exchange(
        ep_count, lambda peer: chosen.at[peer], lambda me, d: raw.at[me], row_send, row_recv
    )
    raw[ep] = chosen[ep]
    for c in copies:
        c.wait()
    squares = jnp.zeros((block.shape[0], 1), jnp.float32)
    for q in range(ep_count):
        wide = raw[q].astype(jnp.float32)
        squares = squares + jnp.sum(wide * wide, axis=1, keepdims=True)
    scale = lax.rsqrt(squares / features + EPS)
    for q in range(ep_count):
        columns = slice(q * width, (q + 1) * width)
        block[:, columns] = (raw[q].astype(jnp.float32) * scale * gain_ref[:, columns]).astype(
            jnp.bfloat16
        )
    gather_blocks(n, block, gathered_ref, send_sem, recv_sem, local_sem)


def route_call(terms, residual, selector, gain, n, ep_count):
    tokens, features = terms.shape
    width = features // ep_count
    count = 2 * (n // 2) - 1
    dma = pltpu.SemaphoreType.DMA
    return pl.pallas_call(
        functools.partial(route_kernel, n, ep_count),
        out_shape=(
            jax.ShapeDtypeStruct((tokens, width), jnp.bfloat16),
            jax.ShapeDtypeStruct((n, CAP, features), jnp.bfloat16),
        ),
        in_specs=[VMEM] * 4,
        out_specs=(VMEM, ANY),
        scratch_shapes=[
            pltpu.VMEM((ep_count - 1, tokens, width), jnp.bfloat16),
            pltpu.VMEM((ep_count, CAP, width), jnp.bfloat16),
            pltpu.VMEM((ep_count, CAP, width), jnp.bfloat16),
            pltpu.VMEM((CAP, features), jnp.bfloat16),
            dma((ep_count - 1,)),
            dma((ep_count - 1,)),
            dma((ep_count - 1,)),
            dma((ep_count - 1,)),
            dma((count,)),
            dma((count,)),
            dma,
        ],
        compiler_params=pltpu.CompilerParams(
            collective_id=1, has_side_effects=True, vmem_limit_bytes=16 << 20
        ),
        name="route",
    )(terms, residual, selector, gain)


def combine_kernel(
    n, ep_count, partial_ref, placer_ref, share_ref, out_ref,
    near, passed, far, sums, slots,
    near_send, near_recv, far_send, far_recv, slot_send, slot_recv,
):
    greet(n, ep_count)
    me, high, low, partner, m = cp_place(n)
    ep = lax.axis_index("ep")
    width = out_ref.shape[1]
    near_copies = []
    for d in [*range(1, m), 0]:
        c = pltpu.make_async_remote_copy(
            src_ref=partial_ref.at[lax.rem(high + d, m) * 2 + 1 - low],
            dst_ref=near.at[d],
            send_sem=near_send.at[d],
            recv_sem=near_recv.at[d],
            device_id={"cp": partner},
        )
        c.start()
        near_copies.append(c)
    far_copies = []
    for d in range(1, m):
        near_copies[d - 1].wait_recv()
        target = lax.rem(high + d, m) * 2 + low
        for q in range(ep_count):
            columns = slice(q * width, (q + 1) * width)
            passed[d - 1, :, columns] = (
                partial_ref[target, :, columns].astype(jnp.float32)
                + near[d, :, columns].astype(jnp.float32)
            ).astype(jnp.bfloat16)
        c = pltpu.make_async_remote_copy(
            src_ref=passed.at[d - 1],
            dst_ref=far.at[d - 1],
            send_sem=far_send.at[d - 1],
            recv_sem=far_recv.at[d - 1],
            device_id={"cp": target},
        )
        c.start()
        far_copies.append(c)
    near_copies[m - 1].wait_recv()
    for c in far_copies:
        c.wait_recv()
    for q in range(ep_count):
        columns = slice(q * width, (q + 1) * width)
        total = partial_ref[me, :, columns].astype(jnp.float32) + near[0, :, columns].astype(
            jnp.float32
        )
        for d in range(1, m):
            total = total + far[d - 1, :, columns].astype(jnp.float32)
        sums[q] = total.astype(jnp.bfloat16)
    copies = ep_exchange(
        ep_count, lambda peer: sums.at[peer], lambda mine, d: slots.at[mine], slot_send, slot_recv
    )
    slots[ep] = sums[ep]
    for c in copies:
        c.wait()
    mix = jnp.zeros(out_ref.shape, jnp.float32)
    for e in range(ep_count):
        mix = mix + share_ref[e] * jnp.dot(
            placer_ref[e], slots[e], preferred_element_type=jnp.float32
        )
    out_ref[...] = mix.astype(jnp.bfloat16)
    for c in near_copies + far_copies:
        c.wait_send()


def combine_call(partial, placer, share, n, ep_count):
    features = partial.shape[2]
    tokens = placer.shape[1]
    width = features // ep_count
    m = n // 2
    dma = pltpu.SemaphoreType.DMA
    block_bytes = 2 * 48 * features
    return pl.pallas_call(
        functools.partial(combine_kernel, n, ep_count),
        out_shape=jax.ShapeDtypeStruct((tokens, width), jnp.bfloat16),
        in_specs=[VMEM] * 3,
        out_specs=VMEM,
        scratch_shapes=[
            pltpu.VMEM((m, CAP, features), jnp.bfloat16),
            pltpu.VMEM((m - 1, CAP, features), jnp.bfloat16),
            pltpu.VMEM((m - 1, CAP, features), jnp.bfloat16),
            pltpu.VMEM((ep_count, CAP, width), jnp.bfloat16),
            pltpu.VMEM((ep_count, CAP, width), jnp.bfloat16),
            dma((m,)),
            dma((m,)),
            dma((m - 1,)),
            dma((m - 1,)),
            dma((ep_count - 1,)),
            dma((ep_count - 1,)),
        ],
        compiler_params=pltpu.CompilerParams(
            collective_id=2,
            has_side_effects=True,
            vmem_limit_bytes=(n + 3 * m) * block_bytes + (8 << 20),
        ),
        name="combine",
    )(partial, placer, share)


def expert_kernel(
    n, ep_count, terms_ref, residual_ref, selector_ref, gain_ref, placer_ref, share_ref,
    gate_hbm, up_hbm, down_hbm,
    hidden_ref, out_ref,
    gate, up, down, landed, chosen, raw, gathered, rows, active, parts, near, far, sums, slots,
    load_sem, term_send, term_recv, row_send, row_recv, block_send, block_recv,
    near_send, near_recv, far_send, far_recv, slot_send, slot_recv,
):
    loads = []
    for index, (source, target) in enumerate([(gate_hbm, gate), (up_hbm, up), (down_hbm, down)]):
        c = pltpu.make_async_copy(source.at[0], target, load_sem.at[index])
        c.start()
        loads.append(c)
    greet(n, ep_count)
    me, high, low, partner, m = cp_place(n)
    ep = lax.axis_index("ep")
    width = hidden_ref.shape[1]
    features = width * ep_count
    units = gate.shape[1]

    def share_of(ref, index):
        return ref.at[:, pl.ds(pl.multiple_of(index * width, 128), width)]

    copies = ep_exchange(
        ep_count,
        lambda peer: share_of(terms_ref, peer),
        lambda mine, d: landed.at[d - 1],
        term_send,
        term_recv,
    )
    total = share_of(residual_ref, ep)[...].astype(jnp.float32) + share_of(terms_ref, ep)[
        ...
    ].astype(jnp.float32)
    for d, c in enumerate(copies):
        c.wait()
        total = total + landed[d].astype(jnp.float32)
    hidden = total.astype(jnp.bfloat16)
    hidden_ref[...] = hidden
    for e in range(ep_count):
        chosen[e] = jnp.dot(
            selector_ref[e], hidden, preferred_element_type=jnp.float32
        ).astype(jnp.bfloat16)
    copies = ep_exchange(
        ep_count, lambda peer: chosen.at[peer], lambda mine, d: raw.at[mine], row_send, row_recv
    )
    raw[ep] = chosen[ep]
    for c in copies:
        c.wait()
    squares = jnp.zeros((raw.shape[1], 1), jnp.float32)
    for q in range(ep_count):
        wide = raw[q].astype(jnp.float32)
        squares = squares + jnp.sum(wide * wide, axis=1, keepdims=True)
    scale = lax.rsqrt(squares / features + EPS)
    for q in range(ep_count):
        columns = slice(q * width, (q + 1) * width)
        gathered[me, :, columns] = (
            raw[q].astype(jnp.float32) * scale * gain_ref[:, columns]
        ).astype(jnp.bfloat16)

    def block_copy(index, sem_at, peer):
        return pltpu.make_async_remote_copy(
            src_ref=gathered.at[index],
            dst_ref=gathered.at[index],
            send_sem=block_send.at[sem_at],
            recv_sem=block_recv.at[sem_at],
            device_id={"cp": peer},
        )

    def place(d):
        return lax.rem(high + m - d, m)

    sent = []

    def send(c):
        c.start()
        sent.append(c)

    send(block_copy(me, 0, partner))
    for d in range(1, m):
        send(block_copy(me, d, lax.rem(high + d, m) * 2 + low))

    def relay(d):
        source = place(d) * 2 + low
        block_copy(source, d, partner).wait_recv()
        send(block_copy(source, m - 1 + d, partner))

    def multiply(d):
        pair = pl.ds(place(d) * 2, 2)
        block_rows = 2 * gathered.shape[1]
        for q in range(ep_count):
            columns = slice(q * width, (q + 1) * width)
            rows[:, columns] = (
                gathered[pair, :, columns]
                .astype(jnp.float32)
                .reshape(block_rows, width)
                .astype(jnp.bfloat16)
            )
        if d == 0:
            loads[0].wait()
            loads[1].wait()

        def unit_tile(j, carry):
            columns = pl.ds(pl.multiple_of(j * 256, 256), 256)
            gated = jnp.dot(rows[...], gate[:, columns], preferred_element_type=jnp.float32)
            lifted = jnp.dot(rows[...], up[:, columns], preferred_element_type=jnp.float32)
            active[:, columns] = (jax.nn.silu(gated) * lifted).astype(jnp.bfloat16)
            return carry

        lax.fori_loop(0, units // 256, unit_tile, 0)
        if d == 0:
            loads[2].wait()

        def feature_tile(j, carry):
            columns = pl.ds(pl.multiple_of(j * 512, 512), 512)
            term = jnp.dot(active[...], down[:, columns], preferred_element_type=jnp.float32)
            parts[pair, :, columns] = term.reshape(2, block_rows // 2, 512).astype(jnp.bfloat16)
            return carry

        lax.fori_loop(0, features // 512, feature_tile, 0)

    def near_copy(d):
        return pltpu.make_async_remote_copy(
            src_ref=parts.at[place(d) * 2 + 1 - low],
            dst_ref=near.at[d],
            send_sem=near_send.at[d],
            recv_sem=near_recv.at[d],
            device_id={"cp": partner},
        )

    far_copies = []

    def pass_on(d):
        near_copy(d).wait_recv()
        target = place(d) * 2 + low
        for q in range(ep_count):
            columns = slice(q * width, (q + 1) * width)
            parts[target, :, columns] = (
                parts[target, :, columns].astype(jnp.float32)
                + near[d, :, columns].astype(jnp.float32)
            ).astype(jnp.bfloat16)
        c = pltpu.make_async_remote_copy(
            src_ref=parts.at[target],
            dst_ref=far.at[d - 1],
            send_sem=far_send.at[d - 1],
            recv_sem=far_recv.at[d - 1],
            device_id={"cp": target},
        )
        send(c)
        far_copies.append(c)

    for d in range(m):
        if d + 1 < m:
            relay(d + 1)
        if d == 0:
            block_copy(partner, 0, partner).wait_recv()
        else:
            block_copy(place(d) * 2 + 1 - low, m - 1 + d, partner).wait_recv()
        multiply(d)
        send(near_copy(d))
        if d >= 2:
            pass_on(d - 1)
    if m > 1:
        pass_on(m - 1)
    near_copy(0).wait_recv()
    for c in far_copies:
        c.wait_recv()
    for q in range(ep_count):
        columns = slice(q * width, (q + 1) * width)
        total = parts[me, :, columns].astype(jnp.float32) + near[0, :, columns].astype(
            jnp.float32
        )
        for d in range(1, m):
            total = total + far[d - 1, :, columns].astype(jnp.float32)
        sums[q] = total.astype(jnp.bfloat16)
    copies = ep_exchange(
        ep_count, lambda peer: sums.at[peer], lambda mine, d: slots.at[mine], slot_send, slot_recv
    )
    slots[ep] = sums[ep]
    for c in copies:
        c.wait()
    mix = jnp.zeros(out_ref.shape, jnp.float32)
    for e in range(ep_count):
        mix = mix + share_ref[e] * jnp.dot(
            placer_ref[e], slots[e], preferred_element_type=jnp.float32
        )
    out_ref[...] = mix.astype(jnp.bfloat16)
    for c in sent:
        c.wait_send()


VMEM_MOST = 67_043_328


def expert_bytes(n, tokens, features, units, ep_count):
    width = features // ep_count
    blocks = n + n + n // 2 + n // 2 - 1 + 4 + 2
    return 2 * (
        3 * features * units
        + blocks * CAP * features
        + 2 * tokens * features
        + (ep_count + 1) * tokens * width
        + 2 * CAP * units
    ) + (4 << 20)


def expert_call(
    terms, residual, selector, gain, placer, share, gate_weight, up_weight, down_weight, n, ep_count
):
    tokens, features = terms.shape
    width = features // ep_count
    units = gate_weight.shape[2]
    m = n // 2
    dma = pltpu.SemaphoreType.DMA
    half = jnp.bfloat16
    ep_sems = [dma((ep_count - 1,))] * 2
    return pl.pallas_call(
        functools.partial(expert_kernel, n, ep_count),
        out_shape=(
            jax.ShapeDtypeStruct((tokens, width), half),
            jax.ShapeDtypeStruct((tokens, width), half),
        ),
        in_specs=[VMEM] * 6 + [ANY] * 3,
        out_specs=(VMEM, VMEM),
        scratch_shapes=[
            pltpu.VMEM((features, units), half),
            pltpu.VMEM((features, units), half),
            pltpu.VMEM((units, features), half),
            pltpu.VMEM((ep_count - 1, tokens, width), half),
            pltpu.VMEM((ep_count, CAP, width), half),
            pltpu.VMEM((ep_count, CAP, width), half),
            pltpu.VMEM((n, CAP, features), half),
            pltpu.VMEM((2 * CAP, features), half),
            pltpu.VMEM((2 * CAP, units), half),
            pltpu.VMEM((n, CAP, features), half),
            pltpu.VMEM((m, CAP, features), half),
            pltpu.VMEM((m - 1, CAP, features), half),
            pltpu.VMEM((ep_count, CAP, width), half),
            pltpu.VMEM((ep_count, CAP, width), half),
            dma((3,)),
            *ep_sems,
            *ep_sems,
            dma((2 * m - 1,)),
            dma((2 * m - 1,)),
            dma((m,)),
            dma((m,)),
            dma((m - 1,)),
            dma((m - 1,)),
            *ep_sems,
        ],
        compiler_params=pltpu.CompilerParams(
            collective_id=3, has_side_effects=True, vmem_limit_bytes=VMEM_MOST
        ),
        name="experts",
    )(terms, residual, selector, gain, placer, share, gate_weight, up_weight, down_weight)


def expert_hidden(rows_in, gate_weight, up_weight):
    gated = jnp.dot(rows_in, gate_weight[0], preferred_element_type=jnp.float32)
    lifted = jnp.dot(rows_in, up_weight[0], preferred_element_type=jnp.float32)
    return (jax.nn.silu(gated) * lifted).astype(jnp.bfloat16)


def local(
    residual,
    queries,
    key_proj,
    value_proj,
    out_weight,
    norm_gain,
    doc_ids,
    block_order,
    expert_ids,
    route_logits,
    gate_weight,
    up_weight,
    down_weight,
):
    tokens, features = residual.shape
    group_size = queries.shape[1] // HD
    score_scale = 1.0 / math.sqrt(HD)
    cp_rank = lax.axis_index("cp")
    n = lax.axis_size("cp")
    ep_count = lax.axis_size("ep")

    pairs = gather_call(jnp.concatenate([key_proj, value_proj], axis=1), n)
    pairs = pairs.reshape(n * tokens, 2 * HD)
    all_keys, all_values = pairs[:, :HD], pairs[:, HD:]
    row = jnp.arange(tokens, dtype=jnp.int32)
    all_pos = (block_order[:, None] * tokens + row[None, :]).reshape(n * tokens)
    all_docs = jnp.take(doc_ids.reshape(n, tokens), block_order, axis=0).reshape(n * tokens)
    placed = lax.dynamic_slice_in_dim(block_order, cp_rank, 1)[0]
    own_pos = placed * tokens + row
    own_docs = lax.dynamic_slice_in_dim(doc_ids, placed * tokens, tokens)
    allowed = (all_docs[None, :] == own_docs[:, None]) & (all_pos[None, :] <= own_pos[:, None])

    query_rows = queries.reshape(tokens * group_size, HD)
    scores = lax.dot_general(
        query_rows, all_keys, (((1,), (1,)), ((), ())), preferred_element_type=jnp.float32
    )
    scores = scores.reshape(tokens, group_size, n * tokens) * score_scale
    scores = jnp.where(allowed[:, None, :], scores, NEG)
    row_max = jnp.max(scores, axis=2)
    weights = jnp.where(allowed[:, None, :], jnp.exp(scores - row_max[:, :, None]), 0.0)
    row_total = jnp.sum(weights, axis=2)
    value_mix = jnp.dot(
        weights.astype(jnp.bfloat16).reshape(tokens * group_size, n * tokens),
        all_values,
        preferred_element_type=jnp.float32,
    ).reshape(tokens, group_size, HD)
    attended = (value_mix / row_total[:, :, None]).reshape(tokens, group_size * HD)
    projected = jnp.dot(
        attended.astype(jnp.bfloat16), out_weight, preferred_element_type=jnp.float32
    ).astype(jnp.bfloat16)

    logit_gap = route_logits[:, 1] - route_logits[:, 0]
    first_share = 1.0 / (1.0 + jnp.exp(logit_gap))
    second_share = 1.0 / (1.0 + jnp.exp(-logit_gap))
    experts = jnp.arange(ep_count, dtype=jnp.int32)[:, None] * gate_weight.shape[0]
    is_first = expert_ids[None, :, 0] == experts
    is_second = expert_ids[None, :, 1] == experts
    member = (is_first | is_second).astype(jnp.int32)
    slot = jnp.cumsum(member, axis=1) - member
    slot_ids = jnp.arange(CAP, dtype=jnp.int32)
    selector = (
        (slot[:, None, :] == slot_ids[None, :, None]) & (member[:, None, :] == 1)
    ).astype(jnp.bfloat16)
    placer = (
        (slot[:, :, None] == slot_ids[None, None, :]) & (member[:, :, None] == 1)
    ).astype(jnp.bfloat16)
    share = jnp.where(is_first, first_share[None], 0.0) + jnp.where(
        is_second, second_share[None], 0.0
    )

    if expert_bytes(n, tokens, features, gate_weight.shape[2], ep_count) <= VMEM_MOST:
        return expert_call(
            projected, residual, selector, norm_gain.reshape(1, features), placer,
            share[:, :, None], gate_weight, up_weight, down_weight, n, ep_count,
        )
    hidden_state, packed = route_call(
        projected, residual, selector, norm_gain.reshape(1, features), n, ep_count
    )
    hidden = expert_hidden(packed.reshape(n * CAP, features), gate_weight, up_weight)
    terms = jnp.dot(hidden, down_weight[0], preferred_element_type=jnp.float32)
    terms = terms.astype(jnp.bfloat16).reshape(n, CAP, features)
    expert_mix = combine_call(terms, placer, share[:, :, None], n, ep_count)
    return (hidden_state, expert_mix)


def solution(mesh):
    return jax.shard_map(
        local,
        mesh=mesh,
        in_specs=(
            P("cp", None),
            P("cp", "ep"),
            P("cp", "ep"),
            P("cp", "ep"),
            P("ep", None),
            P(),
            P(),
            P(),
            P("cp", None),
            P("cp", None),
            P("ep", None, "cp"),
            P("ep", None, "cp"),
            P("ep", "cp", None),
        ),
        out_specs=(P("cp", "ep"), P("cp", "ep")),
        check_vma=False,
    )
```

```python
import functools
import math

import jax
import jax.numpy as jnp
from jax import lax
from jax.experimental import pallas as pl
from jax.experimental.pallas import tpu as pltpu
from jax.sharding import PartitionSpec as P

HD = 128
CAP = 40


EPS = 1e-05
NEG = -1e30
VMEM = pl.BlockSpec(memory_space=pltpu.VMEM)
ANY = pl.BlockSpec(memory_space=pl.ANY)


def cp_place(n):
    me = lax.axis_index("cp")
    low = lax.rem(me, 2)
    return me, me // 2, low, me + 1 - 2 * low, n // 2


def greet(n, ep_count):
    me, high, low, partner, m = cp_place(n)
    barrier = pltpu.get_barrier_semaphore()
    pl.semaphore_signal(barrier, inc=1, device_id={"cp": partner})
    for d in range(1, m):
        peer = lax.rem(high + d, m) * 2 + low
        pl.semaphore_signal(barrier, inc=1, device_id={"cp": peer})
    ep = lax.axis_index("ep")
    for d in range(1, ep_count):
        pl.semaphore_signal(barrier, inc=1, device_id={"ep": lax.rem(ep + d, ep_count)})
    pl.semaphore_wait(barrier, m + ep_count - 1)


def gather_blocks(n, block, out_ref, send_sem, recv_sem, local_sem):
    gather_start(n, block, out_ref, send_sem, recv_sem, local_sem)()


def gather_start(n, block, out_ref, send_sem, recv_sem, local_sem):
    me, high, low, partner, m = cp_place(n)

    def copy(src, index, sem_at, peer):
        return pltpu.make_async_remote_copy(
            src_ref=src,
            dst_ref=out_ref.at[index],
            send_sem=send_sem.at[sem_at],
            recv_sem=recv_sem.at[sem_at],
            device_id={"cp": peer},
        )

    own = pltpu.make_async_copy(block, out_ref.at[me], local_sem)
    own.start()
    sent = []
    for d in range(1, m):
        c = copy(block, me, d, lax.rem(high + d, m) * 2 + low)
        c.start()
        sent.append(c)
    c = copy(block, me, 0, partner)
    c.start()
    sent.append(c)

    def end():
        for d in range(1, m):
            source = lax.rem(high + m - d, m) * 2 + low
            copy(block, source, d, partner).wait_recv()
            c = copy(out_ref.at[source], source, m - 1 + d, partner)
            c.start()
            sent.append(c)
        copy(block, partner, 0, partner).wait_recv()
        for d in range(1, m):
            source = lax.rem(high + m - d, m) * 2 + 1 - low
            copy(block, source, m - 1 + d, partner).wait_recv()
        for c in sent:
            c.wait_send()
        own.wait()

    return end


def attend_kernel(
    n, q_ref, k_ref, v_ref, docs_ref, order_ref, weight_hbm, terms_ref,
    keys, values, mask, attended, weight,
    load_sem, key_send, key_recv, key_local, value_send, value_recv, value_local,
):
    load = pltpu.make_async_copy(weight_hbm, weight, load_sem)
    load.start()
    greet(n, 1)
    me = lax.axis_index("cp")
    tokens = q_ref.shape[0]
    key_end = gather_start(n, k_ref, keys, key_send, key_recv, key_local)
    value_end = gather_start(n, v_ref, values, value_send, value_recv, value_local)
    own = order_ref[me]
    square = (tokens, tokens)
    own_docs = jnp.broadcast_to(docs_ref[pl.ds(own, 1), :], square).T
    below = lax.broadcasted_iota(jnp.int32, square, 0) + own * tokens
    across = lax.broadcasted_iota(jnp.int32, square, 1)
    for i in range(n):
        at = order_ref[i]
        docs = jnp.broadcast_to(docs_ref[pl.ds(at, 1), :], square)
        allowed = (docs == own_docs) & (across + at * tokens <= below)
        mask[:, i * tokens : (i + 1) * tokens] = jnp.where(allowed, 1.0, 0.0)
    key_end()
    value_end()
    all_keys = keys[...].reshape(n * tokens, HD)
    all_values = values[...].reshape(n * tokens, HD)
    score_scale = 1.0 / math.sqrt(HD)
    for h in range(q_ref.shape[1] // HD):
        columns = slice(h * HD, (h + 1) * HD)
        scores = lax.dot_general(
            q_ref[:, columns],
            all_keys,
            (((1,), (1,)), ((), ())),
            preferred_element_type=jnp.float32,
        )
        allowed = mask[...] > 0.5
        scores = jnp.where(allowed, scores * score_scale, NEG)
        weights = jnp.exp(scores - jnp.max(scores, axis=1, keepdims=True))
        weights = jnp.where(allowed, weights, 0.0)
        row_total = jnp.sum(weights, axis=1, keepdims=True)
        mixed = jnp.dot(
            weights.astype(jnp.bfloat16), all_values, preferred_element_type=jnp.float32
        )
        attended[:, columns] = (mixed / row_total).astype(jnp.bfloat16)
    load.wait()

    def feature_tile(j, carry):
        columns = pl.ds(pl.multiple_of(j * 512, 512), 512)
        terms_ref[:, columns] = jnp.dot(
            attended[...], weight[:, columns], preferred_element_type=jnp.float32
        ).astype(jnp.bfloat16)
        return carry

    lax.fori_loop(0, terms_ref.shape[1] // 512, feature_tile, 0)


def attend_call(queries, key_proj, value_proj, doc_ids, block_order, out_weight, n):
    tokens, heads_width = queries.shape
    features = out_weight.shape[1]
    count = 2 * (n // 2) - 1
    dma = pltpu.SemaphoreType.DMA
    half = jnp.bfloat16
    return pl.pallas_call(
        functools.partial(attend_kernel, n),
        out_shape=jax.ShapeDtypeStruct((tokens, features), half),
        in_specs=[VMEM] * 4 + [pl.BlockSpec(memory_space=pltpu.SMEM), ANY],
        out_specs=VMEM,
        scratch_shapes=[
            pltpu.VMEM((n, tokens, HD), half),
            pltpu.VMEM((n, tokens, HD), half),
            pltpu.VMEM((tokens, n * tokens), jnp.float32),
            pltpu.VMEM((tokens, heads_width), half),
            pltpu.VMEM(out_weight.shape, half),
            dma,
            dma((count,)),
            dma((count,)),
            dma,
            dma((count,)),
            dma((count,)),
            dma,
        ],
        compiler_params=pltpu.CompilerParams(
            collective_id=0, has_side_effects=True, vmem_limit_bytes=40 << 20
        ),
        name="attend",
    )(queries, key_proj, value_proj, doc_ids.reshape(n, tokens), block_order, out_weight)


def ep_exchange(ep_count, source_of, target_of, send_sem, recv_sem):
    ep = lax.axis_index("ep")
    copies = []
    for d in range(1, ep_count):
        peer = lax.rem(ep + d, ep_count)
        c = pltpu.make_async_remote_copy(
            src_ref=source_of(peer),
            dst_ref=target_of(ep, d),
            send_sem=send_sem.at[d - 1],
            recv_sem=recv_sem.at[d - 1],
            device_id={"ep": peer},
        )
        c.start()
        copies.append(c)
    return copies


def route_kernel(
    n, ep_count, terms_ref, residual_ref, selector_ref, gain_ref,
    hidden_ref, gathered_ref,
    landed, chosen, raw, block,
    term_send, term_recv, row_send, row_recv, send_sem, recv_sem, local_sem,
):
    greet(n, ep_count)
    ep = lax.axis_index("ep")
    width = hidden_ref.shape[1]
    features = width * ep_count

    def share_of(ref, index):
        return ref.at[:, pl.ds(pl.multiple_of(index * width, 128), width)]

    copies = ep_exchange(
        ep_count,
        lambda peer: share_of(terms_ref, peer),
        lambda me, d: landed.at[d - 1],
        term_send,
        term_recv,
    )
    total = share_of(residual_ref, ep)[...].astype(jnp.float32) + share_of(terms_ref, ep)[
        ...
    ].astype(jnp.float32)
    for d, c in enumerate(copies):
        c.wait()
        total = total + landed[d].astype(jnp.float32)
    hidden = total.astype(jnp.bfloat16)
    hidden_ref[...] = hidden
    for e in range(ep_count):
        chosen[e] = jnp.dot(
            selector_ref[e], hidden, preferred_element_type=jnp.float32
        ).astype(jnp.bfloat16)
    copies = ep_exchange(
        ep_count, lambda peer: chosen.at[peer], lambda me, d: raw.at[me], row_send, row_recv
    )
    raw[ep] = chosen[ep]
    for c in copies:
        c.wait()
    squares = jnp.zeros((block.shape[0], 1), jnp.float32)
    for q in range(ep_count):
        wide = raw[q].astype(jnp.float32)
        squares = squares + jnp.sum(wide * wide, axis=1, keepdims=True)
    scale = lax.rsqrt(squares / features + EPS)
    for q in range(ep_count):
        columns = slice(q * width, (q + 1) * width)
        block[:, columns] = (raw[q].astype(jnp.float32) * scale * gain_ref[:, columns]).astype(
            jnp.bfloat16
        )
    gather_blocks(n, block, gathered_ref, send_sem, recv_sem, local_sem)


def route_call(terms, residual, selector, gain, n, ep_count):
    tokens, features = terms.shape
    width = features // ep_count
    count = 2 * (n // 2) - 1
    dma = pltpu.SemaphoreType.DMA
    return pl.pallas_call(
        functools.partial(route_kernel, n, ep_count),
        out_shape=(
            jax.ShapeDtypeStruct((tokens, width), jnp.bfloat16),
            jax.ShapeDtypeStruct((n, CAP, features), jnp.bfloat16),
        ),
        in_specs=[VMEM] * 4,
        out_specs=(VMEM, ANY),
        scratch_shapes=[
            pltpu.VMEM((ep_count - 1, tokens, width), jnp.bfloat16),
            pltpu.VMEM((ep_count, CAP, width), jnp.bfloat16),
            pltpu.VMEM((ep_count, CAP, width), jnp.bfloat16),
            pltpu.VMEM((CAP, features), jnp.bfloat16),
            dma((ep_count - 1,)),
            dma((ep_count - 1,)),
            dma((ep_count - 1,)),
            dma((ep_count - 1,)),
            dma((count,)),
            dma((count,)),
            dma,
        ],
        compiler_params=pltpu.CompilerParams(
            collective_id=1, has_side_effects=True, vmem_limit_bytes=16 << 20
        ),
        name="route",
    )(terms, residual, selector, gain)


def combine_kernel(
    n, ep_count, partial_ref, placer_ref, share_ref, out_ref,
    near, passed, far, sums, slots,
    near_send, near_recv, far_send, far_recv, slot_send, slot_recv,
):
    greet(n, ep_count)
    me, high, low, partner, m = cp_place(n)
    ep = lax.axis_index("ep")
    width = out_ref.shape[1]
    near_copies = []
    for d in [*range(1, m), 0]:
        c = pltpu.make_async_remote_copy(
            src_ref=partial_ref.at[lax.rem(high + d, m) * 2 + 1 - low],
            dst_ref=near.at[d],
            send_sem=near_send.at[d],
            recv_sem=near_recv.at[d],
            device_id={"cp": partner},
        )
        c.start()
        near_copies.append(c)
    far_copies = []
    for d in range(1, m):
        near_copies[d - 1].wait_recv()
        target = lax.rem(high + d, m) * 2 + low
        for q in range(ep_count):
            columns = slice(q * width, (q + 1) * width)
            passed[d - 1, :, columns] = (
                partial_ref[target, :, columns].astype(jnp.float32)
                + near[d, :, columns].astype(jnp.float32)
            ).astype(jnp.bfloat16)
        c = pltpu.make_async_remote_copy(
            src_ref=passed.at[d - 1],
            dst_ref=far.at[d - 1],
            send_sem=far_send.at[d - 1],
            recv_sem=far_recv.at[d - 1],
            device_id={"cp": target},
        )
        c.start()
        far_copies.append(c)
    near_copies[m - 1].wait_recv()
    for c in far_copies:
        c.wait_recv()
    for q in range(ep_count):
        columns = slice(q * width, (q + 1) * width)
        total = partial_ref[me, :, columns].astype(jnp.float32) + near[0, :, columns].astype(
            jnp.float32
        )
        for d in range(1, m):
            total = total + far[d - 1, :, columns].astype(jnp.float32)
        sums[q] = total.astype(jnp.bfloat16)
    copies = ep_exchange(
        ep_count, lambda peer: sums.at[peer], lambda mine, d: slots.at[mine], slot_send, slot_recv
    )
    slots[ep] = sums[ep]
    for c in copies:
        c.wait()
    mix = jnp.zeros(out_ref.shape, jnp.float32)
    for e in range(ep_count):
        mix = mix + share_ref[e] * jnp.dot(
            placer_ref[e], slots[e], preferred_element_type=jnp.float32
        )
    out_ref[...] = mix.astype(jnp.bfloat16)
    for c in near_copies + far_copies:
        c.wait_send()


def combine_call(partial, placer, share, n, ep_count):
    features = partial.shape[2]
    tokens = placer.shape[1]
    width = features // ep_count
    m = n // 2
    dma = pltpu.SemaphoreType.DMA
    block_bytes = 2 * 48 * features
    return pl.pallas_call(
        functools.partial(combine_kernel, n, ep_count),
        out_shape=jax.ShapeDtypeStruct((tokens, width), jnp.bfloat16),
        in_specs=[VMEM] * 3,
        out_specs=VMEM,
        scratch_shapes=[
            pltpu.VMEM((m, CAP, features), jnp.bfloat16),
            pltpu.VMEM((m - 1, CAP, features), jnp.bfloat16),
            pltpu.VMEM((m - 1, CAP, features), jnp.bfloat16),
            pltpu.VMEM((ep_count, CAP, width), jnp.bfloat16),
            pltpu.VMEM((ep_count, CAP, width), jnp.bfloat16),
            dma((m,)),
            dma((m,)),
            dma((m - 1,)),
            dma((m - 1,)),
            dma((ep_count - 1,)),
            dma((ep_count - 1,)),
        ],
        compiler_params=pltpu.CompilerParams(
            collective_id=2,
            has_side_effects=True,
            vmem_limit_bytes=(n + 3 * m) * block_bytes + (8 << 20),
        ),
        name="combine",
    )(partial, placer, share)


def expert_kernel(
    n, ep_count, terms_ref, residual_ref, selector_ref, gain_ref, placer_ref, share_ref,
    gate_hbm, up_hbm, down_hbm,
    hidden_ref, out_ref,
    gate, up, down, landed, halves, others, chosen, raw, gathered, rows, active, parts, near, far, sums, slots,
    load_sem, term_send, term_recv, half_send, half_recv, row_send, row_recv, block_send, block_recv,
    near_send, near_recv, far_send, far_recv, slot_send, slot_recv,
):
    loads = []
    for index, (source, target) in enumerate([(gate_hbm, gate), (up_hbm, up), (down_hbm, down)]):
        c = pltpu.make_async_copy(source.at[0], target, load_sem.at[index])
        c.start()
        loads.append(c)
    greet(n, ep_count)
    me, high, low, partner, m = cp_place(n)
    ep = lax.axis_index("ep")
    width = hidden_ref.shape[1]
    features = width * ep_count
    units = gate.shape[1]

    def share_of(ref, index):
        return ref.at[:, pl.ds(pl.multiple_of(index * width, 128), width)]

    side = lax.rem(ep, 2)
    sibling = ep + 1 - 2 * side
    pairs = ep_count // 2

    def pair_at(d):
        return lax.rem(ep // 2 + d, pairs)

    copies = []
    for d in [*range(1, pairs), 0]:
        c = pltpu.make_async_remote_copy(
            src_ref=share_of(terms_ref, pair_at(d) * 2 + 1 - side),
            dst_ref=landed.at[d],
            send_sem=term_send.at[d],
            recv_sem=term_recv.at[d],
            device_id={"ep": sibling},
        )
        c.start()
        copies.append(c)
    summed = []
    for d in range(1, pairs):
        copies[d - 1].wait_recv()
        target = pair_at(d) * 2 + side
        halves[d - 1] = (
            share_of(terms_ref, target)[...].astype(jnp.float32) + landed[d].astype(jnp.float32)
        ).astype(jnp.bfloat16)
        c = pltpu.make_async_remote_copy(
            src_ref=halves.at[d - 1],
            dst_ref=others.at[d - 1],
            send_sem=half_send.at[d - 1],
            recv_sem=half_recv.at[d - 1],
            device_id={"ep": target},
        )
        c.start()
        summed.append(c)
    copies[pairs - 1].wait_recv()
    total = share_of(residual_ref, ep)[...].astype(jnp.float32) + share_of(terms_ref, ep)[
        ...
    ].astype(jnp.float32)
    total = total + landed[0].astype(jnp.float32)
    for d, c in enumerate(summed):
        c.wait_recv()
        total = total + others[d].astype(jnp.float32)
    copies_near_ep = copies
    hidden = total.astype(jnp.bfloat16)
    hidden_ref[...] = hidden
    for e in range(ep_count):
        chosen[e] = jnp.dot(
            selector_ref[e], hidden, preferred_element_type=jnp.float32
        ).astype(jnp.bfloat16)
    copies = ep_exchange(
        ep_count, lambda peer: chosen.at[peer], lambda mine, d: raw.at[mine], row_send, row_recv
    )
    raw[ep] = chosen[ep]
    for c in copies:
        c.wait()
    squares = jnp.zeros((raw.shape[1], 1), jnp.float32)
    for q in range(ep_count):
        wide = raw[q].astype(jnp.float32)
        squares = squares + jnp.sum(wide * wide, axis=1, keepdims=True)
    scale = lax.rsqrt(squares / features + EPS)
    for q in range(ep_count):
        columns = slice(q * width, (q + 1) * width)
        gathered[me, :, columns] = (
            raw[q].astype(jnp.float32) * scale * gain_ref[:, columns]
        ).astype(jnp.bfloat16)

    def block_copy(index, sem_at, peer):
        return pltpu.make_async_remote_copy(
            src_ref=gathered.at[index],
            dst_ref=gathered.at[index],
            send_sem=block_send.at[sem_at],
            recv_sem=block_recv.at[sem_at],
            device_id={"cp": peer},
        )

    def place(d):
        return lax.rem(high + m - d, m)

    sent = []

    def send(c):
        c.start()
        sent.append(c)

    send(block_copy(me, 0, partner))
    for d in range(1, m):
        send(block_copy(me, d, lax.rem(high + d, m) * 2 + low))

    def relay(d):
        source = place(d) * 2 + low
        block_copy(source, d, partner).wait_recv()
        send(block_copy(source, m - 1 + d, partner))

    def multiply(d):
        pair = pl.ds(place(d) * 2, 2)
        block_rows = 2 * gathered.shape[1]
        for q in range(ep_count):
            columns = slice(q * width, (q + 1) * width)
            rows[:, columns] = (
                gathered[pair, :, columns]
                .astype(jnp.float32)
                .reshape(block_rows, width)
                .astype(jnp.bfloat16)
            )
        if d == 0:
            loads[0].wait()
            loads[1].wait()

        def unit_tile(j, carry):
            columns = pl.ds(pl.multiple_of(j * 256, 256), 256)
            gated = jnp.dot(rows[...], gate[:, columns], preferred_element_type=jnp.float32)
            lifted = jnp.dot(rows[...], up[:, columns], preferred_element_type=jnp.float32)
            active[:, columns] = (jax.nn.silu(gated) * lifted).astype(jnp.bfloat16)
            return carry

        lax.fori_loop(0, units // 256, unit_tile, 0)
        if d == 0:
            loads[2].wait()

        def feature_tile(j, carry):
            columns = pl.ds(pl.multiple_of(j * 512, 512), 512)
            term = jnp.dot(active[...], down[:, columns], preferred_element_type=jnp.float32)
            parts[pair, :, columns] = term.reshape(2, block_rows // 2, 512).astype(jnp.bfloat16)
            return carry

        lax.fori_loop(0, features // 512, feature_tile, 0)

    def near_copy(d):
        return pltpu.make_async_remote_copy(
            src_ref=parts.at[place(d) * 2 + 1 - low],
            dst_ref=near.at[d],
            send_sem=near_send.at[d],
            recv_sem=near_recv.at[d],
            device_id={"cp": partner},
        )

    far_copies = []

    def pass_on(d):
        near_copy(d).wait_recv()
        target = place(d) * 2 + low
        for q in range(ep_count):
            columns = slice(q * width, (q + 1) * width)
            parts[target, :, columns] = (
                parts[target, :, columns].astype(jnp.float32)
                + near[d, :, columns].astype(jnp.float32)
            ).astype(jnp.bfloat16)
        c = pltpu.make_async_remote_copy(
            src_ref=parts.at[target],
            dst_ref=far.at[d - 1],
            send_sem=far_send.at[d - 1],
            recv_sem=far_recv.at[d - 1],
            device_id={"cp": target},
        )
        send(c)
        far_copies.append(c)

    for d in range(m):
        if d + 1 < m:
            relay(d + 1)
        if d == 0:
            block_copy(partner, 0, partner).wait_recv()
        else:
            block_copy(place(d) * 2 + 1 - low, m - 1 + d, partner).wait_recv()
        multiply(d)
        send(near_copy(d))
        if d >= 2:
            pass_on(d - 1)
    if m > 1:
        pass_on(m - 1)
    near_copy(0).wait_recv()
    for c in far_copies:
        c.wait_recv()
    for q in range(ep_count):
        columns = slice(q * width, (q + 1) * width)
        total = parts[me, :, columns].astype(jnp.float32) + near[0, :, columns].astype(
            jnp.float32
        )
        for d in range(1, m):
            total = total + far[d - 1, :, columns].astype(jnp.float32)
        sums[q] = total.astype(jnp.bfloat16)
    copies = ep_exchange(
        ep_count, lambda peer: sums.at[peer], lambda mine, d: slots.at[mine], slot_send, slot_recv
    )
    slots[ep] = sums[ep]
    for c in copies:
        c.wait()
    mix = jnp.zeros(out_ref.shape, jnp.float32)
    for e in range(ep_count):
        mix = mix + share_ref[e] * jnp.dot(
            placer_ref[e], slots[e], preferred_element_type=jnp.float32
        )
    out_ref[...] = mix.astype(jnp.bfloat16)
    for c in sent + summed:
        c.wait_send()
    for c in copies_near_ep:
        c.wait_send()


VMEM_MOST = 67_043_328


def expert_bytes(n, tokens, features, units, ep_count):
    width = features // ep_count
    blocks = n + n + n // 2 + n // 2 - 1 + 4 + 2
    return 2 * (
        3 * features * units
        + blocks * CAP * features
        + 2 * tokens * features
        + (ep_count + 2) * tokens * width
        + 2 * CAP * units
    ) + (4 << 20)


def expert_call(
    terms, residual, selector, gain, placer, share, gate_weight, up_weight, down_weight, n, ep_count
):
    tokens, features = terms.shape
    width = features // ep_count
    units = gate_weight.shape[2]
    m = n // 2
    dma = pltpu.SemaphoreType.DMA
    half = jnp.bfloat16
    ep_sems = [dma((ep_count - 1,))] * 2
    return pl.pallas_call(
        functools.partial(expert_kernel, n, ep_count),
        out_shape=(
            jax.ShapeDtypeStruct((tokens, width), half),
            jax.ShapeDtypeStruct((tokens, width), half),
        ),
        in_specs=[VMEM] * 6 + [ANY] * 3,
        out_specs=(VMEM, VMEM),
        scratch_shapes=[
            pltpu.VMEM((features, units), half),
            pltpu.VMEM((features, units), half),
            pltpu.VMEM((units, features), half),
            pltpu.VMEM((ep_count // 2, tokens, width), half),
            pltpu.VMEM((ep_count // 2 - 1, tokens, width), half),
            pltpu.VMEM((ep_count // 2 - 1, tokens, width), half),
            pltpu.VMEM((ep_count, CAP, width), half),
            pltpu.VMEM((ep_count, CAP, width), half),
            pltpu.VMEM((n, CAP, features), half),
            pltpu.VMEM((2 * CAP, features), half),
            pltpu.VMEM((2 * CAP, units), half),
            pltpu.VMEM((n, CAP, features), half),
            pltpu.VMEM((m, CAP, features), half),
            pltpu.VMEM((m - 1, CAP, features), half),
            pltpu.VMEM((ep_count, CAP, width), half),
            pltpu.VMEM((ep_count, CAP, width), half),
            dma((3,)),
            dma((ep_count // 2,)),
            dma((ep_count // 2,)),
            dma((ep_count // 2 - 1,)),
            dma((ep_count // 2 - 1,)),
            *ep_sems,
            dma((2 * m - 1,)),
            dma((2 * m - 1,)),
            dma((m,)),
            dma((m,)),
            dma((m - 1,)),
            dma((m - 1,)),
            *ep_sems,
        ],
        compiler_params=pltpu.CompilerParams(
            collective_id=3, has_side_effects=True, vmem_limit_bytes=VMEM_MOST
        ),
        name="experts",
    )(terms, residual, selector, gain, placer, share, gate_weight, up_weight, down_weight)


def expert_hidden(rows_in, gate_weight, up_weight):
    gated = jnp.dot(rows_in, gate_weight[0], preferred_element_type=jnp.float32)
    lifted = jnp.dot(rows_in, up_weight[0], preferred_element_type=jnp.float32)
    return (jax.nn.silu(gated) * lifted).astype(jnp.bfloat16)


def local(
    residual,
    queries,
    key_proj,
    value_proj,
    out_weight,
    norm_gain,
    doc_ids,
    block_order,
    expert_ids,
    route_logits,
    gate_weight,
    up_weight,
    down_weight,
):
    tokens, features = residual.shape
    n = lax.axis_size("cp")
    ep_count = lax.axis_size("ep")

    projected = attend_call(
        queries, key_proj, value_proj, doc_ids, block_order, out_weight, n
    )

    logit_gap = route_logits[:, 1] - route_logits[:, 0]
    first_share = 1.0 / (1.0 + jnp.exp(logit_gap))
    second_share = 1.0 / (1.0 + jnp.exp(-logit_gap))
    experts = jnp.arange(ep_count, dtype=jnp.int32)[:, None] * gate_weight.shape[0]
    is_first = expert_ids[None, :, 0] == experts
    is_second = expert_ids[None, :, 1] == experts
    member = (is_first | is_second).astype(jnp.int32)
    slot = jnp.cumsum(member, axis=1) - member
    slot_ids = jnp.arange(CAP, dtype=jnp.int32)
    selector = (
        (slot[:, None, :] == slot_ids[None, :, None]) & (member[:, None, :] == 1)
    ).astype(jnp.bfloat16)
    placer = (
        (slot[:, :, None] == slot_ids[None, None, :]) & (member[:, :, None] == 1)
    ).astype(jnp.bfloat16)
    share = jnp.where(is_first, first_share[None], 0.0) + jnp.where(
        is_second, second_share[None], 0.0
    )

    if expert_bytes(n, tokens, features, gate_weight.shape[2], ep_count) <= VMEM_MOST:
        return expert_call(
            projected, residual, selector, norm_gain.reshape(1, features), placer,
            share[:, :, None], gate_weight, up_weight, down_weight, n, ep_count,
        )
    hidden_state, packed = route_call(
        projected, residual, selector, norm_gain.reshape(1, features), n, ep_count
    )
    hidden = expert_hidden(packed.reshape(n * CAP, features), gate_weight, up_weight)
    terms = jnp.dot(hidden, down_weight[0], preferred_element_type=jnp.float32)
    terms = terms.astype(jnp.bfloat16).reshape(n, CAP, features)
    expert_mix = combine_call(terms, placer, share[:, :, None], n, ep_count)
    return (hidden_state, expert_mix)


def solution(mesh):
    return jax.shard_map(
        local,
        mesh=mesh,
        in_specs=(
            P("cp", None),
            P("cp", "ep"),
            P("cp", "ep"),
            P("cp", "ep"),
            P("ep", None),
            P(),
            P(),
            P(),
            P("cp", None),
            P("cp", None),
            P("ep", None, "cp"),
            P("ep", None, "cp"),
            P("ep", "cp", None),
        ),
        out_specs=(P("cp", "ep"), P("cp", "ep")),
        check_vma=False,
    )
```

```python
import functools
import math

import jax
import jax.numpy as jnp
from jax import lax
from jax.experimental import pallas as pl
from jax.experimental.pallas import tpu as pltpu
from jax.sharding import PartitionSpec as P

HD = 128
CAP = 40


EPS = 1e-05
NEG = -1e30
VMEM = pl.BlockSpec(memory_space=pltpu.VMEM)
ANY = pl.BlockSpec(memory_space=pl.ANY)


def cp_place(n):
    me = lax.axis_index("cp")
    low = lax.rem(me, 2)
    return me, me // 2, low, me + 1 - 2 * low, n // 2


def greet(n, ep_count):
    me, high, low, partner, m = cp_place(n)
    barrier = pltpu.get_barrier_semaphore()
    pl.semaphore_signal(barrier, inc=1, device_id={"cp": partner})
    for d in range(1, m):
        peer = lax.rem(high + d, m) * 2 + low
        pl.semaphore_signal(barrier, inc=1, device_id={"cp": peer})
    ep = lax.axis_index("ep")
    for d in range(1, ep_count):
        pl.semaphore_signal(barrier, inc=1, device_id={"ep": lax.rem(ep + d, ep_count)})
    pl.semaphore_wait(barrier, m + ep_count - 1)


def gather_blocks(n, block, out_ref, send_sem, recv_sem, local_sem):
    gather_start(n, block, out_ref, send_sem, recv_sem, local_sem)()


def gather_start(n, block, out_ref, send_sem, recv_sem, local_sem):
    me, high, low, partner, m = cp_place(n)

    def copy(src, index, sem_at, peer):
        return pltpu.make_async_remote_copy(
            src_ref=src,
            dst_ref=out_ref.at[index],
            send_sem=send_sem.at[sem_at],
            recv_sem=recv_sem.at[sem_at],
            device_id={"cp": peer},
        )

    own = pltpu.make_async_copy(block, out_ref.at[me], local_sem)
    own.start()
    sent = []
    for d in range(1, m):
        c = copy(block, me, d, lax.rem(high + d, m) * 2 + low)
        c.start()
        sent.append(c)
    c = copy(block, me, 0, partner)
    c.start()
    sent.append(c)

    def end():
        for d in range(1, m):
            source = lax.rem(high + m - d, m) * 2 + low
            copy(block, source, d, partner).wait_recv()
            c = copy(out_ref.at[source], source, m - 1 + d, partner)
            c.start()
            sent.append(c)
        copy(block, partner, 0, partner).wait_recv()
        for d in range(1, m):
            source = lax.rem(high + m - d, m) * 2 + 1 - low
            copy(block, source, m - 1 + d, partner).wait_recv()
        for c in sent:
            c.wait_send()
        own.wait()

    return end


def attend_kernel(
    n, q_ref, k_ref, v_ref, docs_ref, order_ref, weight_hbm, terms_ref,
    keys, values, mask, attended, weight,
    load_sem, key_send, key_recv, key_local, value_send, value_recv, value_local,
):
    load = pltpu.make_async_copy(weight_hbm, weight, load_sem)
    load.start()
    greet(n, 1)
    me = lax.axis_index("cp")
    tokens = q_ref.shape[0]
    key_end = gather_start(n, k_ref, keys, key_send, key_recv, key_local)
    value_end = gather_start(n, v_ref, values, value_send, value_recv, value_local)
    own = order_ref[me]
    square = (tokens, tokens)
    own_docs = jnp.broadcast_to(docs_ref[pl.ds(own, 1), :], square).T
    below = lax.broadcasted_iota(jnp.int32, square, 0) + own * tokens
    across = lax.broadcasted_iota(jnp.int32, square, 1)
    for i in range(n):
        at = order_ref[i]
        docs = jnp.broadcast_to(docs_ref[pl.ds(at, 1), :], square)
        allowed = (docs == own_docs) & (across + at * tokens <= below)
        mask[:, i * tokens : (i + 1) * tokens] = jnp.where(allowed, 1.0, 0.0)
    key_end()
    value_end()
    all_keys = keys[...].reshape(n * tokens, HD)
    all_values = values[...].reshape(n * tokens, HD)
    score_scale = 1.0 / math.sqrt(HD)
    for h in range(q_ref.shape[1] // HD):
        columns = slice(h * HD, (h + 1) * HD)
        scores = lax.dot_general(
            q_ref[:, columns],
            all_keys,
            (((1,), (1,)), ((), ())),
            preferred_element_type=jnp.float32,
        )
        allowed = mask[...] > 0.5
        scores = jnp.where(allowed, scores * score_scale, NEG)
        weights = jnp.exp(scores - jnp.max(scores, axis=1, keepdims=True))
        weights = jnp.where(allowed, weights, 0.0)
        row_total = jnp.sum(weights, axis=1, keepdims=True)
        mixed = jnp.dot(
            weights.astype(jnp.bfloat16), all_values, preferred_element_type=jnp.float32
        )
        attended[:, columns] = (mixed / row_total).astype(jnp.bfloat16)
    load.wait()

    def feature_tile(j, carry):
        columns = pl.ds(pl.multiple_of(j * 512, 512), 512)
        terms_ref[:, columns] = jnp.dot(
            attended[...], weight[:, columns], preferred_element_type=jnp.float32
        ).astype(jnp.bfloat16)
        return carry

    lax.fori_loop(0, terms_ref.shape[1] // 512, feature_tile, 0)


def attend_call(queries, key_proj, value_proj, doc_ids, block_order, out_weight, n):
    tokens, heads_width = queries.shape
    features = out_weight.shape[1]
    count = 2 * (n // 2) - 1
    dma = pltpu.SemaphoreType.DMA
    half = jnp.bfloat16
    return pl.pallas_call(
        functools.partial(attend_kernel, n),
        out_shape=jax.ShapeDtypeStruct((tokens, features), half),
        in_specs=[VMEM] * 4 + [pl.BlockSpec(memory_space=pltpu.SMEM), ANY],
        out_specs=VMEM,
        scratch_shapes=[
            pltpu.VMEM((n, tokens, HD), half),
            pltpu.VMEM((n, tokens, HD), half),
            pltpu.VMEM((tokens, n * tokens), jnp.float32),
            pltpu.VMEM((tokens, heads_width), half),
            pltpu.VMEM(out_weight.shape, half),
            dma,
            dma((count,)),
            dma((count,)),
            dma,
            dma((count,)),
            dma((count,)),
            dma,
        ],
        compiler_params=pltpu.CompilerParams(
            collective_id=0, has_side_effects=True, vmem_limit_bytes=40 << 20
        ),
        name="attend",
    )(queries, key_proj, value_proj, doc_ids.reshape(n, tokens), block_order, out_weight)


def ep_exchange(ep_count, source_of, target_of, send_sem, recv_sem):
    ep = lax.axis_index("ep")
    copies = []
    for d in range(1, ep_count):
        peer = lax.rem(ep + d, ep_count)
        c = pltpu.make_async_remote_copy(
            src_ref=source_of(peer),
            dst_ref=target_of(ep, d),
            send_sem=send_sem.at[d - 1],
            recv_sem=recv_sem.at[d - 1],
            device_id={"ep": peer},
        )
        c.start()
        copies.append(c)
    return copies


def route_kernel(
    n, ep_count, terms_ref, residual_ref, selector_ref, gain_ref,
    hidden_ref, gathered_ref,
    landed, chosen, raw, block,
    term_send, term_recv, row_send, row_recv, send_sem, recv_sem, local_sem,
):
    greet(n, ep_count)
    ep = lax.axis_index("ep")
    width = hidden_ref.shape[1]
    features = width * ep_count

    def share_of(ref, index):
        return ref.at[:, pl.ds(pl.multiple_of(index * width, 128), width)]

    copies = ep_exchange(
        ep_count,
        lambda peer: share_of(terms_ref, peer),
        lambda me, d: landed.at[d - 1],
        term_send,
        term_recv,
    )
    total = share_of(residual_ref, ep)[...].astype(jnp.float32) + share_of(terms_ref, ep)[
        ...
    ].astype(jnp.float32)
    for d, c in enumerate(copies):
        c.wait()
        total = total + landed[d].astype(jnp.float32)
    hidden = total.astype(jnp.bfloat16)
    hidden_ref[...] = hidden
    for e in range(ep_count):
        chosen[e] = jnp.dot(
            selector_ref[e], hidden, preferred_element_type=jnp.float32
        ).astype(jnp.bfloat16)
    copies = ep_exchange(
        ep_count, lambda peer: chosen.at[peer], lambda me, d: raw.at[me], row_send, row_recv
    )
    raw[ep] = chosen[ep]
    for c in copies:
        c.wait()
    squares = jnp.zeros((block.shape[0], 1), jnp.float32)
    for q in range(ep_count):
        wide = raw[q].astype(jnp.float32)
        squares = squares + jnp.sum(wide * wide, axis=1, keepdims=True)
    scale = lax.rsqrt(squares / features + EPS)
    for q in range(ep_count):
        columns = slice(q * width, (q + 1) * width)
        block[:, columns] = (raw[q].astype(jnp.float32) * scale * gain_ref[:, columns]).astype(
            jnp.bfloat16
        )
    gather_blocks(n, block, gathered_ref, send_sem, recv_sem, local_sem)


def route_call(terms, residual, selector, gain, n, ep_count):
    tokens, features = terms.shape
    width = features // ep_count
    count = 2 * (n // 2) - 1
    dma = pltpu.SemaphoreType.DMA
    return pl.pallas_call(
        functools.partial(route_kernel, n, ep_count),
        out_shape=(
            jax.ShapeDtypeStruct((tokens, width), jnp.bfloat16),
            jax.ShapeDtypeStruct((n, CAP, features), jnp.bfloat16),
        ),
        in_specs=[VMEM] * 4,
        out_specs=(VMEM, ANY),
        scratch_shapes=[
            pltpu.VMEM((ep_count - 1, tokens, width), jnp.bfloat16),
            pltpu.VMEM((ep_count, CAP, width), jnp.bfloat16),
            pltpu.VMEM((ep_count, CAP, width), jnp.bfloat16),
            pltpu.VMEM((CAP, features), jnp.bfloat16),
            dma((ep_count - 1,)),
            dma((ep_count - 1,)),
            dma((ep_count - 1,)),
            dma((ep_count - 1,)),
            dma((count,)),
            dma((count,)),
            dma,
        ],
        compiler_params=pltpu.CompilerParams(
            collective_id=1, has_side_effects=True, vmem_limit_bytes=16 << 20
        ),
        name="route",
    )(terms, residual, selector, gain)


def combine_kernel(
    n, ep_count, partial_ref, placer_ref, share_ref, out_ref,
    near, passed, far, sums, slots,
    near_send, near_recv, far_send, far_recv, slot_send, slot_recv,
):
    greet(n, ep_count)
    me, high, low, partner, m = cp_place(n)
    ep = lax.axis_index("ep")
    width = out_ref.shape[1]
    near_copies = []
    for d in [*range(1, m), 0]:
        c = pltpu.make_async_remote_copy(
            src_ref=partial_ref.at[lax.rem(high + d, m) * 2 + 1 - low],
            dst_ref=near.at[d],
            send_sem=near_send.at[d],
            recv_sem=near_recv.at[d],
            device_id={"cp": partner},
        )
        c.start()
        near_copies.append(c)
    far_copies = []
    for d in range(1, m):
        near_copies[d - 1].wait_recv()
        target = lax.rem(high + d, m) * 2 + low
        for q in range(ep_count):
            columns = slice(q * width, (q + 1) * width)
            passed[d - 1, :, columns] = (
                partial_ref[target, :, columns].astype(jnp.float32)
                + near[d, :, columns].astype(jnp.float32)
            ).astype(jnp.bfloat16)
        c = pltpu.make_async_remote_copy(
            src_ref=passed.at[d - 1],
            dst_ref=far.at[d - 1],
            send_sem=far_send.at[d - 1],
            recv_sem=far_recv.at[d - 1],
            device_id={"cp": target},
        )
        c.start()
        far_copies.append(c)
    near_copies[m - 1].wait_recv()
    for c in far_copies:
        c.wait_recv()
    for q in range(ep_count):
        columns = slice(q * width, (q + 1) * width)
        total = partial_ref[me, :, columns].astype(jnp.float32) + near[0, :, columns].astype(
            jnp.float32
        )
        for d in range(1, m):
            total = total + far[d - 1, :, columns].astype(jnp.float32)
        sums[q] = total.astype(jnp.bfloat16)
    copies = ep_exchange(
        ep_count, lambda peer: sums.at[peer], lambda mine, d: slots.at[mine], slot_send, slot_recv
    )
    slots[ep] = sums[ep]
    for c in copies:
        c.wait()
    mix = jnp.zeros(out_ref.shape, jnp.float32)
    for e in range(ep_count):
        mix = mix + share_ref[e] * jnp.dot(
            placer_ref[e], slots[e], preferred_element_type=jnp.float32
        )
    out_ref[...] = mix.astype(jnp.bfloat16)
    for c in near_copies + far_copies:
        c.wait_send()


def combine_call(partial, placer, share, n, ep_count):
    features = partial.shape[2]
    tokens = placer.shape[1]
    width = features // ep_count
    m = n // 2
    dma = pltpu.SemaphoreType.DMA
    block_bytes = 2 * 48 * features
    return pl.pallas_call(
        functools.partial(combine_kernel, n, ep_count),
        out_shape=jax.ShapeDtypeStruct((tokens, width), jnp.bfloat16),
        in_specs=[VMEM] * 3,
        out_specs=VMEM,
        scratch_shapes=[
            pltpu.VMEM((m, CAP, features), jnp.bfloat16),
            pltpu.VMEM((m - 1, CAP, features), jnp.bfloat16),
            pltpu.VMEM((m - 1, CAP, features), jnp.bfloat16),
            pltpu.VMEM((ep_count, CAP, width), jnp.bfloat16),
            pltpu.VMEM((ep_count, CAP, width), jnp.bfloat16),
            dma((m,)),
            dma((m,)),
            dma((m - 1,)),
            dma((m - 1,)),
            dma((ep_count - 1,)),
            dma((ep_count - 1,)),
        ],
        compiler_params=pltpu.CompilerParams(
            collective_id=2,
            has_side_effects=True,
            vmem_limit_bytes=(n + 3 * m) * block_bytes + (8 << 20),
        ),
        name="combine",
    )(partial, placer, share)


def expert_kernel(
    n, ep_count, terms_ref, residual_ref, selector_ref, gain_ref, placer_ref, share_ref,
    gate_hbm, up_hbm, down_hbm,
    hidden_ref, out_ref,
    gate, up, down, own, landed, halves, others, chosen, raw, gathered, rows, active, parts, near, far, sums, slots,
    load_sem, own_sem, term_send, term_recv, half_send, half_recv, row_send, row_recv, block_send, block_recv,
    near_send, near_recv, far_send, far_recv, slot_send, slot_recv,
):
    loads = []
    for index, (source, target) in enumerate([(gate_hbm, gate), (up_hbm, up), (down_hbm, down)]):
        c = pltpu.make_async_copy(source.at[0], target, load_sem.at[index])
        c.start()
        loads.append(c)
    greet(n, ep_count)
    me, high, low, partner, m = cp_place(n)
    ep = lax.axis_index("ep")
    width = hidden_ref.shape[1]
    features = width * ep_count
    units = gate.shape[1]

    def share_of(ref, index):
        return ref.at[:, pl.ds(pl.multiple_of(index * width, 128), width)]

    own_load = pltpu.make_async_copy(share_of(residual_ref, ep), own, own_sem)
    own_load.start()
    side = lax.rem(ep, 2)
    sibling = ep + 1 - 2 * side
    pairs = ep_count // 2

    def pair_at(d):
        return lax.rem(ep // 2 + d, pairs)

    copies = []
    for d in [*range(1, pairs), 0]:
        c = pltpu.make_async_remote_copy(
            src_ref=share_of(terms_ref, pair_at(d) * 2 + 1 - side),
            dst_ref=landed.at[d],
            send_sem=term_send.at[d],
            recv_sem=term_recv.at[d],
            device_id={"ep": sibling},
        )
        c.start()
        copies.append(c)
    summed = []
    for d in range(1, pairs):
        copies[d - 1].wait_recv()
        target = pair_at(d) * 2 + side
        halves[d - 1] = (
            share_of(terms_ref, target)[...].astype(jnp.float32) + landed[d].astype(jnp.float32)
        ).astype(jnp.bfloat16)
        c = pltpu.make_async_remote_copy(
            src_ref=halves.at[d - 1],
            dst_ref=others.at[d - 1],
            send_sem=half_send.at[d - 1],
            recv_sem=half_recv.at[d - 1],
            device_id={"ep": target},
        )
        c.start()
        summed.append(c)
    copies[pairs - 1].wait_recv()
    own_load.wait()
    total = own[...].astype(jnp.float32) + share_of(terms_ref, ep)[
        ...
    ].astype(jnp.float32)
    total = total + landed[0].astype(jnp.float32)
    for d, c in enumerate(summed):
        c.wait_recv()
        total = total + others[d].astype(jnp.float32)
    copies_near_ep = copies
    hidden = total.astype(jnp.bfloat16)
    hidden_ref[...] = hidden
    for e in range(ep_count):
        chosen[e] = jnp.dot(
            selector_ref[e], hidden, preferred_element_type=jnp.float32
        ).astype(jnp.bfloat16)
    copies = ep_exchange(
        ep_count, lambda peer: chosen.at[peer], lambda mine, d: raw.at[mine], row_send, row_recv
    )
    raw[ep] = chosen[ep]
    for c in copies:
        c.wait()
    squares = jnp.zeros((raw.shape[1], 1), jnp.float32)
    for q in range(ep_count):
        wide = raw[q].astype(jnp.float32)
        squares = squares + jnp.sum(wide * wide, axis=1, keepdims=True)
    scale = lax.rsqrt(squares / features + EPS)
    for q in range(ep_count):
        columns = slice(q * width, (q + 1) * width)
        gathered[me, :, columns] = (
            raw[q].astype(jnp.float32) * scale * gain_ref[:, columns]
        ).astype(jnp.bfloat16)

    def block_copy(index, sem_at, peer):
        return pltpu.make_async_remote_copy(
            src_ref=gathered.at[index],
            dst_ref=gathered.at[index],
            send_sem=block_send.at[sem_at],
            recv_sem=block_recv.at[sem_at],
            device_id={"cp": peer},
        )

    def place(d):
        return lax.rem(high + m - d, m)

    sent = []

    def send(c):
        c.start()
        sent.append(c)

    send(block_copy(me, 0, partner))
    for d in range(1, m):
        send(block_copy(me, d, lax.rem(high + d, m) * 2 + low))

    def relay(d):
        source = place(d) * 2 + low
        block_copy(source, d, partner).wait_recv()
        send(block_copy(source, m - 1 + d, partner))

    def multiply(d):
        pair = pl.ds(place(d) * 2, 2)
        block_rows = 2 * gathered.shape[1]
        for q in range(ep_count):
            columns = slice(q * width, (q + 1) * width)
            rows[:, columns] = (
                gathered[pair, :, columns]
                .astype(jnp.float32)
                .reshape(block_rows, width)
                .astype(jnp.bfloat16)
            )
        if d == 0:
            loads[0].wait()
            loads[1].wait()

        def unit_tile(j, carry):
            columns = pl.ds(pl.multiple_of(j * 256, 256), 256)
            gated = jnp.dot(rows[...], gate[:, columns], preferred_element_type=jnp.float32)
            lifted = jnp.dot(rows[...], up[:, columns], preferred_element_type=jnp.float32)
            active[:, columns] = (jax.nn.silu(gated) * lifted).astype(jnp.bfloat16)
            return carry

        lax.fori_loop(0, units // 256, unit_tile, 0)
        if d == 0:
            loads[2].wait()

        def feature_tile(j, carry):
            columns = pl.ds(pl.multiple_of(j * 512, 512), 512)
            term = jnp.dot(active[...], down[:, columns], preferred_element_type=jnp.float32)
            parts[pair, :, columns] = term.reshape(2, block_rows // 2, 512).astype(jnp.bfloat16)
            return carry

        lax.fori_loop(0, features // 512, feature_tile, 0)

    def near_copy(d):
        return pltpu.make_async_remote_copy(
            src_ref=parts.at[place(d) * 2 + 1 - low],
            dst_ref=near.at[d],
            send_sem=near_send.at[d],
            recv_sem=near_recv.at[d],
            device_id={"cp": partner},
        )

    far_copies = []

    def pass_on(d):
        near_copy(d).wait_recv()
        target = place(d) * 2 + low
        for q in range(ep_count):
            columns = slice(q * width, (q + 1) * width)
            parts[target, :, columns] = (
                parts[target, :, columns].astype(jnp.float32)
                + near[d, :, columns].astype(jnp.float32)
            ).astype(jnp.bfloat16)
        c = pltpu.make_async_remote_copy(
            src_ref=parts.at[target],
            dst_ref=far.at[d - 1],
            send_sem=far_send.at[d - 1],
            recv_sem=far_recv.at[d - 1],
            device_id={"cp": target},
        )
        send(c)
        far_copies.append(c)

    for d in range(m):
        if d + 1 < m:
            relay(d + 1)
        if d == 0:
            block_copy(partner, 0, partner).wait_recv()
        else:
            block_copy(place(d) * 2 + 1 - low, m - 1 + d, partner).wait_recv()
        multiply(d)
        if d >= 1:
            send(near_copy(d))
        if d >= 2:
            pass_on(d - 1)
    send(near_copy(0))
    if m > 1:
        pass_on(m - 1)
    near_copy(0).wait_recv()
    for c in far_copies:
        c.wait_recv()
    for q in range(ep_count):
        columns = slice(q * width, (q + 1) * width)
        total = parts[me, :, columns].astype(jnp.float32) + near[0, :, columns].astype(
            jnp.float32
        )
        for d in range(1, m):
            total = total + far[d - 1, :, columns].astype(jnp.float32)
        sums[q] = total.astype(jnp.bfloat16)
    copies = ep_exchange(
        ep_count, lambda peer: sums.at[peer], lambda mine, d: slots.at[mine], slot_send, slot_recv
    )
    slots[ep] = sums[ep]
    for c in copies:
        c.wait()
    mix = jnp.zeros(out_ref.shape, jnp.float32)
    for e in range(ep_count):
        mix = mix + share_ref[e] * jnp.dot(
            placer_ref[e], slots[e], preferred_element_type=jnp.float32
        )
    out_ref[...] = mix.astype(jnp.bfloat16)
    for c in sent + summed:
        c.wait_send()
    for c in copies_near_ep:
        c.wait_send()


VMEM_MOST = 67_043_328


def expert_bytes(n, tokens, features, units, ep_count):
    width = features // ep_count
    blocks = n + n + n // 2 + n // 2 - 1 + 4 + 2
    return 2 * (
        3 * features * units
        + blocks * CAP * features
        + 2 * tokens * features
        + (ep_count + 2) * tokens * width
        + 2 * CAP * units
    ) + (4 << 20)


def expert_call(
    terms, residual, selector, gain, placer, share, gate_weight, up_weight, down_weight, n, ep_count
):
    tokens, features = terms.shape
    width = features // ep_count
    units = gate_weight.shape[2]
    m = n // 2
    dma = pltpu.SemaphoreType.DMA
    half = jnp.bfloat16
    ep_sems = [dma((ep_count - 1,))] * 2
    return pl.pallas_call(
        functools.partial(expert_kernel, n, ep_count),
        out_shape=(
            jax.ShapeDtypeStruct((tokens, width), half),
            jax.ShapeDtypeStruct((tokens, width), half),
        ),
        in_specs=[VMEM, ANY] + [VMEM] * 4 + [ANY] * 3,
        out_specs=(VMEM, VMEM),
        scratch_shapes=[
            pltpu.VMEM((features, units), half),
            pltpu.VMEM((features, units), half),
            pltpu.VMEM((units, features), half),
            pltpu.VMEM((tokens, width), half),
            pltpu.VMEM((ep_count // 2, tokens, width), half),
            pltpu.VMEM((ep_count // 2 - 1, tokens, width), half),
            pltpu.VMEM((ep_count // 2 - 1, tokens, width), half),
            pltpu.VMEM((ep_count, CAP, width), half),
            pltpu.VMEM((ep_count, CAP, width), half),
            pltpu.VMEM((n, CAP, features), half),
            pltpu.VMEM((2 * CAP, features), half),
            pltpu.VMEM((2 * CAP, units), half),
            pltpu.VMEM((n, CAP, features), half),
            pltpu.VMEM((m, CAP, features), half),
            pltpu.VMEM((m - 1, CAP, features), half),
            pltpu.VMEM((ep_count, CAP, width), half),
            pltpu.VMEM((ep_count, CAP, width), half),
            dma((3,)),
            dma,
            dma((ep_count // 2,)),
            dma((ep_count // 2,)),
            dma((ep_count // 2 - 1,)),
            dma((ep_count // 2 - 1,)),
            *ep_sems,
            dma((2 * m - 1,)),
            dma((2 * m - 1,)),
            dma((m,)),
            dma((m,)),
            dma((m - 1,)),
            dma((m - 1,)),
            *ep_sems,
        ],
        compiler_params=pltpu.CompilerParams(
            collective_id=3, has_side_effects=True, vmem_limit_bytes=VMEM_MOST
        ),
        name="experts",
    )(terms, residual, selector, gain, placer, share, gate_weight, up_weight, down_weight)


def expert_hidden(rows_in, gate_weight, up_weight):
    gated = jnp.dot(rows_in, gate_weight[0], preferred_element_type=jnp.float32)
    lifted = jnp.dot(rows_in, up_weight[0], preferred_element_type=jnp.float32)
    return (jax.nn.silu(gated) * lifted).astype(jnp.bfloat16)


def local(
    residual,
    queries,
    key_proj,
    value_proj,
    out_weight,
    norm_gain,
    doc_ids,
    block_order,
    expert_ids,
    route_logits,
    gate_weight,
    up_weight,
    down_weight,
):
    tokens, features = residual.shape
    n = lax.axis_size("cp")
    ep_count = lax.axis_size("ep")

    projected = attend_call(
        queries, key_proj, value_proj, doc_ids, block_order, out_weight, n
    )

    logit_gap = route_logits[:, 1] - route_logits[:, 0]
    first_share = 1.0 / (1.0 + jnp.exp(logit_gap))
    second_share = 1.0 / (1.0 + jnp.exp(-logit_gap))
    experts = jnp.arange(ep_count, dtype=jnp.int32)[:, None] * gate_weight.shape[0]
    is_first = expert_ids[None, :, 0] == experts
    is_second = expert_ids[None, :, 1] == experts
    member = (is_first | is_second).astype(jnp.int32)
    slot = jnp.cumsum(member, axis=1) - member
    slot_ids = jnp.arange(CAP, dtype=jnp.int32)
    selector = (
        (slot[:, None, :] == slot_ids[None, :, None]) & (member[:, None, :] == 1)
    ).astype(jnp.bfloat16)
    placer = (
        (slot[:, :, None] == slot_ids[None, None, :]) & (member[:, :, None] == 1)
    ).astype(jnp.bfloat16)
    share = jnp.where(is_first, first_share[None], 0.0) + jnp.where(
        is_second, second_share[None], 0.0
    )

    if expert_bytes(n, tokens, features, gate_weight.shape[2], ep_count) <= VMEM_MOST:
        return expert_call(
            projected, residual, selector, norm_gain.reshape(1, features), placer,
            share[:, :, None], gate_weight, up_weight, down_weight, n, ep_count,
        )
    hidden_state, packed = route_call(
        projected, residual, selector, norm_gain.reshape(1, features), n, ep_count
    )
    hidden = expert_hidden(packed.reshape(n * CAP, features), gate_weight, up_weight)
    terms = jnp.dot(hidden, down_weight[0], preferred_element_type=jnp.float32)
    terms = terms.astype(jnp.bfloat16).reshape(n, CAP, features)
    expert_mix = combine_call(terms, placer, share[:, :, None], n, ep_count)
    return (hidden_state, expert_mix)


def solution(mesh):
    return jax.shard_map(
        local,
        mesh=mesh,
        in_specs=(
            P("cp", None),
            P("cp", "ep"),
            P("cp", "ep"),
            P("cp", "ep"),
            P("ep", None),
            P(),
            P(),
            P(),
            P("cp", None),
            P("cp", None),
            P("ep", None, "cp"),
            P("ep", None, "cp"),
            P("ep", "cp", None),
        ),
        out_specs=(P("cp", "ep"), P("cp", "ep")),
        check_vma=False,
    )
```
